256 devices in a mesh: win: 16 (over y, z_lo), space: 16 (over z_hi, x, core).
Axes of the slice: x: 4, y: 4, z: 8 (z_hi: 2, z_lo: 4; z = z_hi * 4 + z_lo), core: 2. Of those that a mesh axis runs over, the one named last changes fastest.
Arguments:
- increment: float32 [16, 64, 256, 256], P('win', 'space'), may hold values from -6 to 6
- multiplier: float32 [16, 64, 256, 256], P('win', 'space'), may hold values from -6 to 6
- obs_dual: float32 [16, 16384], P('win', 'space'), may hold values from -6 to 6
- obs_sites: int32 [16, 3, 16384], P('win'), may hold values from 0 to 255, as said below
- obs_variance: float32 [16, 16384], P('win', 'space'), may hold values from 0.5 to 2
- trajectory: bfloat16 [16, 64, 256, 256], P('win', None, 'space'), may hold values from -6 to 6
- diffusion: float32 [64], replicated, may hold values from 0.05 to 0.2
- drift_rows: float32 [64], replicated, may hold values from -0.25 to 0.25
- drift_cols: float32 [64], replicated, may hold values from -0.25 to 0.25
- spread: float32 [64], replicated, may hold values from 0.5 to 2
- row_factor: float32 [256, 256], replicated, may hold values from -0.375 to 0.375
- col_factor: float32 [256, 256], replicated, may hold values from -0.375 to 0.375
- layer_in: bfloat16 [1024, 64], replicated, may hold values from -0.75 to 0.75
- bias_in: float32 [1024], replicated, may hold values from -4 to 4
- layer_out: bfloat16 [64, 1024], replicated, may hold values from -0.1875 to 0.1875
Outputs:
- state_out: float32 [16, 64, 256, 256], P('win', 'space')
- obs_out: float32 [16, 16384], P('win', 'space')
- mult_out: float32 [16, 64, 256, 256], P('win', 'space')
The draws below stay inside these ranges and needn't reach their ends.
Inputs may be any that keep to these rules, and one draw needn't show every extreme that they name: `obs_sites`: row 0 holds a level below 64, row 1 a first index below 256, row 2 a second index below 256; positions may repeat.
All inputs are finite; a program needn't handle non-finite values.
Results may differ from the reference program's by a relative error of at most 0.0011.
Values sent between devices are 32-bit elements; how exact they have to be, the bound alone decides.
A program may use at most 64 MiB of HBM per device.

```python
import math
import jax
import jax.numpy as jnp
from jax import lax

NX = 256
NY = 256
LEV = 64
HID = 1024
STEPS = 4
SUBWINS = 16
NOBS = 16384


def draw_obs_sites(key, part):
    keys = jax.random.split(jax.random.fold_in(key, 7), 3)
    levels = jax.random.randint(keys[0], (SUBWINS, NOBS), 0, LEV)
    first = jax.random.randint(keys[1], (SUBWINS, NOBS), 0, NX)
    second = jax.random.randint(keys[2], (SUBWINS, NOBS), 0, NY)
    levels = levels.at[:, 0].set(LEV - 1).at[:, 1].set(0)
    first = first.at[:, 0].set(NX - 1).at[:, 1].set(0)
    second = second.at[:, 0].set(NY - 1).at[:, 1].set(0)
    return jnp.stack([levels, first, second], 1).astype(jnp.int32)


def block_levels(key, extent, cuts, low, top_value):
    gain, own = 1.0, jax.random.fold_in(key, 6)
    for axis_at, blocks in cuts:
        heights = jnp.exp(jax.random.uniform(jax.random.fold_in(own, axis_at), (blocks,), jnp.float32, low / len(cuts), top_value / len(cuts)))
        gain = gain * jnp.repeat(heights, extent[axis_at] // blocks).reshape([-1 if axis == axis_at else 1 for axis in range(len(extent))])
    return gain


def bell_draw(rng, shape, width, most, shards=(), held_as=jnp.bfloat16):
    level = block_levels(rng, shape, shards, -0.22, 0.18) if shards else 1.0
    result = jax.random.normal(rng, shape, jnp.float32) * width * level
    return jnp.minimum(jnp.maximum(result, -most), most).astype(held_as)


def setup_inputs(seed: int = 0) -> dict:
    key_list = jax.random.split(jax.random.key(seed), 16)
    return {
        "increment": bell_draw(key_list[0], (SUBWINS, LEV, NX, NY), 1.0, 6.0, ((0, 16), (1, 16)), jnp.float32),
        "multiplier": bell_draw(key_list[1], (SUBWINS, LEV, NX, NY), 1.0, 6.0, ((0, 16), (1, 16)), jnp.float32),
        "obs_dual": bell_draw(key_list[2], (SUBWINS, NOBS), 1.0, 6.0, ((0, 16), (1, 16)), jnp.float32),
        "obs_sites": draw_obs_sites(jax.random.fold_in(key_list[15], 71), 0),
        "obs_variance": jnp.clip(jnp.exp(math.log(2.0) - 1.3862944 * jax.random.uniform(key_list[4], (SUBWINS, NOBS), jnp.float32) ** block_levels(key_list[4], (SUBWINS, NOBS), ((0, 16), (1, 16)), -0.2, 0.2)), 0.5, 2.0),
        "trajectory": bell_draw(key_list[5], (SUBWINS, LEV, NX, NY), 1.0, 6.0, ((0, 16), (2, 16))),
        "diffusion": jnp.clip(jnp.exp(jax.random.uniform(key_list[6], (LEV,), jnp.float32, math.log(0.05), math.log(0.2))), 0.05, 0.2),
        "drift_rows": jnp.clip(jax.random.uniform(key_list[7], (LEV,), jnp.float32, -0.25, 0.25), -0.25, 0.25),
        "drift_cols": jnp.clip(jax.random.uniform(key_list[8], (LEV,), jnp.float32, -0.25, 0.25), -0.25, 0.25),
        "spread": jnp.clip(jnp.exp(jax.random.uniform(key_list[9], (LEV,), jnp.float32, math.log(0.5), math.log(2.0))), 0.5, 2.0),
        "row_factor": bell_draw(key_list[10], (NX, NX), NX ** -0.5, 0.375, (), jnp.float32),
        "col_factor": bell_draw(key_list[11], (NY, NY), NY ** -0.5, 0.375, (), jnp.float32),
        "layer_in": bell_draw(key_list[12], (HID, LEV), LEV ** -0.5, 0.75),
        "bias_in": bell_draw(key_list[13], (HID,), 1.0, 4.0, (), jnp.float32),
        "layer_out": bell_draw(key_list[14], (LEV, HID), HID ** -0.5, 0.1875),
    }


exact_mode = lax.Precision.HIGHEST


def stencil_step(padded, diffusion, drift_rows, drift_cols, direction):
    centre = padded[:, 1:-1, :]
    row_up = padded[:, 2:, :]
    row_down = padded[:, :-2, :]
    widened = jnp.pad(centre, ((0, 0), (0, 0), (1, 1)))
    col_up = widened[:, :, 2:]
    col_down = widened[:, :, :-2]
    mixing = row_up + row_down + col_up + col_down - 4.0 * centre
    carried = drift_rows * (row_up - row_down) + drift_cols * (col_up - col_down)
    return centre + diffusion * mixing - direction * carried


def bf_round(values):
    return lax.optimization_barrier(values.astype(jnp.bfloat16)).astype(jnp.float32)


def network_both(forward_in, backward_in, trajectory, layer_in, bias_in, layer_out):
    levels, row_count, columns = forward_in.shape
    block_rows = min(row_count, max(1, 1024 // columns))
    weight_in = layer_in.astype(jnp.float32)
    weight_out = layer_out.astype(jnp.float32)

    def select(source, first_row):
        piece = lax.dynamic_slice_in_dim(source, first_row, block_rows, 1)
        return piece.reshape(levels, block_rows * columns)

    def visit(block_index, totals):
        first_row = (block_index * block_rows).astype(jnp.int32)
        path = select(trajectory, first_row).astype(jnp.float32)
        activation = jnp.dot(weight_in, path) + bias_in[:, None]
        gating = jax.nn.sigmoid(activation)
        slopes = gating * (1.0 + activation * (1.0 - gating))
        tangent_in = select(forward_in, first_row)
        hidden = bf_round(slopes * jnp.dot(weight_in, bf_round(tangent_in)))
        tangent_out = tangent_in + jnp.dot(weight_out, hidden)
        adjoint_in = select(backward_in, first_row)
        back_hidden = bf_round(slopes * jnp.dot(weight_out.T, bf_round(adjoint_in)))
        adjoint_out = adjoint_in + jnp.dot(weight_in.T, back_hidden)
        shape = (levels, block_rows, columns)
        return (lax.dynamic_update_slice_in_dim(totals[0], tangent_out.reshape(shape), first_row, 1),
                lax.dynamic_update_slice_in_dim(totals[1], adjoint_out.reshape(shape), first_row, 1))

    empty = jnp.zeros(forward_in.shape, jnp.float32)
    return lax.fori_loop(0, row_count // block_rows, visit, (empty, empty))


def correlate(fields, spread, row_factor, col_factor):
    inner = jnp.einsum('xa,lxy->lay', row_factor, fields, precision=exact_mode)
    inner = jnp.einsum('lay,yb->lab', inner, col_factor, precision=exact_mode)
    outer = jnp.einsum('xa,lab->lxb', row_factor, inner, precision=exact_mode)
    outer = jnp.einsum('lxb,yb->lxy', outer, col_factor, precision=exact_mode)
    return (spread * spread)[:, None, None] * outer


def reference(increment, multiplier, obs_dual, obs_sites, obs_variance, trajectory, diffusion, drift_rows, drift_cols, spread, row_factor, col_factor, layer_in, bias_in, layer_out):
    coefs = (diffusion[:, None, None], drift_rows[:, None, None], drift_cols[:, None, None])

    def stepping(fields, direction):
        for repeat in range(STEPS):
            padded = jnp.pad(fields, ((0, 0), (1, 1), (0, 0)))
            fields = stencil_step(padded, coefs[0], coefs[1], coefs[2], direction)
        return fields

    blank = jnp.zeros((1, LEV, NX, NY), jnp.float32)
    previous = jnp.concatenate([blank, increment[:-1]], 0)

    def per_window(window_items):
        prior_one, mult_one, path_one = window_items
        tangent, adjoint = network_both(stepping(prior_one, 1.0), mult_one, path_one, layer_in, bias_in, layer_out)
        return tangent, stepping(adjoint, -1.0)

    forward, backward = lax.map(per_window, (previous, multiplier, trajectory))
    later = jnp.concatenate([backward[1:], blank], 0)
    correlated = lax.map(lambda fields: correlate(fields, spread, row_factor, col_factor), multiplier)
    state_out = (correlated + increment) - forward

    def observe(fields, positions):
        return fields[positions[0], positions[1], positions[2]]

    seen = jax.vmap(observe)(increment, obs_sites)
    obs_out = obs_variance * obs_dual + seen

    def place(duals, positions):
        return jnp.zeros((LEV, NX, NY), jnp.float32).at[positions[0], positions[1], positions[2]].add(duals)

    placed = jax.vmap(place)(obs_dual, obs_sites)
    mult_out = (multiplier - later) + placed
    return state_out, obs_out, mult_out
```

```python
import jax
import jax.numpy as jnp
from jax import lax
from jax.experimental import pallas as pl
from jax.experimental.pallas import tpu as pltpu
from jax.sharding import PartitionSpec as P

STEPS = 4
MESH = pl.DeviceIdType.MESH
F32, BF16 = jnp.float32, jnp.bfloat16
PARTNERS = (8, 12, 10, 14, 9, 13, 11, 15, 4, 6, 2, 5, 7, 3, 1)
BLOCK = 512
LANES = 128


def flip(value, mask):
    for bit in (1, 2, 4, 8):
        if mask & bit:
            value = value + bit * (1 - 2 * lax.rem(lax.div(value, bit), 2))
    return value


def split_two(value):
    high = value.astype(BF16)
    low = (value - high.astype(F32)).astype(BF16)
    return high, low


def dot(a, b):
    return jnp.dot(a, b, preferred_element_type=F32)


def dot_nt(a, b, precision=None):
    return lax.dot_general(
        a, b, (((1,), (1,)), ((), ())), precision=precision, preferred_element_type=F32
    )


def dot_three(a, b):
    return dot(a[0], b[0]) + (dot(a[0], b[1]) + dot(a[1], b[0]))


def stencil(field, diffusion, drift_rows, drift_cols, direction):
    rows, cols = field.shape
    row_id = lax.broadcasted_iota(jnp.int32, field.shape, 0)
    col_id = lax.broadcasted_iota(jnp.int32, field.shape, 1)
    centre = 1.0 - 4.0 * diffusion
    row_up, row_dn = diffusion - direction * drift_rows, diffusion + direction * drift_rows
    col_up, col_dn = diffusion - direction * drift_cols, diffusion + direction * drift_cols
    for _ in range(STEPS):
        up1 = jnp.where(row_id == rows - 1, 0.0, pltpu.roll(field, rows - 1, 0))
        dn1 = jnp.where(row_id == 0, 0.0, pltpu.roll(field, 1, 0))
        up2 = jnp.where(col_id == cols - 1, 0.0, pltpu.roll(field, cols - 1, 1))
        dn2 = jnp.where(col_id == 0, 0.0, pltpu.roll(field, 1, 1))
        field = centre * field + (row_up * up1 + row_dn * dn1) + (col_up * up2 + col_dn * dn2)
    return field


def kernel(
    sites, dual, variance, diffusion, drift_rows, drift_cols, spread, row_factor, col_factor,
    w_in, bias, w_out, inc_any, mult_any, traj_any,
    state_any, obs_out, mult_out_any,
    inc, mult, stepped, traj, path, strip_m, strip_i, slopes, out_b, out_f, slab_b, slab_f,
    before, placed, picked, w_path, w_tangent, w_adjoint, w_in_t, duals, seen, seen_in,
    outs, outm,
    load_sem, store_sem, m_send, m_recv, i_send, i_recv, b_send, b_recv, f_send, f_recv,
    d_send, d_recv, s_send, s_recv, keep_sem,
):
    depth, rows, cols = inc.shape
    chunks, levels, strip, _ = strip_m.shape
    hidden = w_in.shape[0]
    spaces = rows // strip
    w, s = lax.axis_index("win"), lax.axis_index("space")
    wins = lax.axis_size("win")
    after, prior = lax.rem(w + 1, wins), lax.rem(w + wins - 1, wins)
    first = s * depth

    barrier = pltpu.get_barrier_semaphore()
    for p in range(spaces):
        d = flip(s, p)
        for win in (w, after, prior):
            if win is w and p == 0:
                continue
            pl.semaphore_signal(
                barrier, inc=1, device_id={"win": win, "space": d}, device_id_type=MESH
            )

    load_inc = pltpu.make_async_copy(inc_any, inc, load_sem.at[0])
    load_traj = pltpu.make_async_copy(traj_any, traj, load_sem.at[1])
    load_mult = pltpu.make_async_copy(mult_any, mult, load_sem.at[2])
    load_inc.start()
    load_traj.start()
    load_mult.start()

    lane = lax.broadcasted_iota(jnp.int32, (hidden, 2 * levels), 1)
    bias_all = jnp.broadcast_to(bias[...], (2 * levels, hidden)).T
    bias_hi = bias_all.astype(BF16).astype(F32)
    bias_mid = (bias_all - bias_hi).astype(BF16).astype(F32)
    bias_lo = bias_all - bias_hi - bias_mid
    w_in32, w_out32 = w_in[...].astype(F32), w_out[...].astype(F32)
    wide = jnp.concatenate([w_in32, jnp.zeros((hidden, levels), F32)], 1)
    wide = jnp.where(lane == levels, bias_hi, wide)
    wide = jnp.where(lane == levels + 1, bias_mid, wide)
    wide = jnp.where(lane == levels + 2, bias_lo, wide)
    w_path[...] = (0.5 * wide).astype(BF16)
    w_tangent[...] = (0.5 * w_in32).astype(BF16)
    w_adjoint[...] = (0.5 * w_out32.T).astype(BF16)
    w_in_t[...] = w_in32.T.astype(BF16)

    load_inc.wait()

    def step_forward(level, carry):
        at = first + level
        stepped[level] = stencil(
            inc[level], diffusion[at], drift_rows[at], drift_cols[at], 1.0
        )
        return carry

    lax.fori_loop(0, depth, step_forward, 0)

    pl.semaphore_wait(barrier, 3 * spaces - 1)

    def remote(src, dst, send, recv, win, space):
        return pltpu.make_async_remote_copy(
            src_ref=src, dst_ref=dst, send_sem=send, recv_sem=recv,
            device_id={"win": win, "space": space}, device_id_type=MESH,
        )

    def strip_of(d):
        return pl.ds(pl.multiple_of(d * strip, strip), strip)

    def depth_of(d):
        return pl.ds(pl.multiple_of(d * depth, depth), depth)

    def chunk_of(c):
        return pl.ds(c * LANES, LANES)

    def dual_copy(p):
        return remote(dual, duals.at[pl.ds(2 * s, 2)], d_send.at[p], d_recv.at[p], w, flip(s, p))

    def mult_copy(p, c):
        d = flip(s, p)
        return remote(
            mult_any.at[:, strip_of(d), chunk_of(c)], strip_m.at[c, depth_of(s)],
            m_send.at[c, p], m_recv.at[c, p], w, d,
        )

    def inc_copy(p, c):
        d = flip(s, p)
        return remote(
            stepped.at[:, strip_of(d), chunk_of(c)], strip_i.at[c, depth_of(s)],
            i_send.at[c, p], i_recv.at[c, p], after, d,
        )

    def back_copy(p, c):
        d = flip(s, p)
        return remote(
            out_b.at[c, depth_of(d)], slab_b.at[:, strip_of(s), chunk_of(c)],
            b_send.at[c, p], b_recv.at[c, p], prior, d,
        )

    def ahead_copy(p, c):
        d = flip(s, p)
        return remote(
            out_f.at[c, depth_of(d)], slab_f.at[:, strip_of(s), chunk_of(c)],
            f_send.at[c, p], f_recv.at[c, p], w, d,
        )

    def seen_copy(p):
        d = flip(s, p)
        return remote(
            seen.at[pl.ds(2 * d, 2)], seen_in.at[s], s_send.at[p], s_recv.at[p], w, d
        )

    keep_dual = pltpu.make_async_copy(dual, duals.at[pl.ds(2 * s, 2)], keep_sem.at[0])
    keep_seen = pltpu.make_async_copy(seen.at[pl.ds(2 * s, 2)], seen_in.at[s], keep_sem.at[1])

    def keep_mult(c):
        return pltpu.make_async_copy(
            mult_any.at[:, strip_of(s), chunk_of(c)], strip_m.at[c, depth_of(s)],
            keep_sem.at[2 + c],
        )

    def keep_ahead(c):
        return pltpu.make_async_copy(
            out_f.at[c, depth_of(s)], slab_f.at[:, strip_of(s), chunk_of(c)],
            keep_sem.at[2 + chunks + c],
        )

    everyone = PARTNERS + (0,)
    has_prior, has_after = w > 0, w < wins - 1

    keep_dual.start()
    for p in PARTNERS:
        dual_copy(p).start()

    @pl.when(has_prior)
    def _():
        for c in range(chunks):
            for p in PARTNERS:
                mult_copy(p, c).start()
            keep_mult(c).start()

    @pl.when(has_after)
    def _():
        for c in range(chunks):
            for p in everyone:
                inc_copy(p, c).start()

    load_traj.wait()
    for c in range(chunks):
        path[c] = traj[:, :, c * LANES : (c + 1) * LANES].astype(F32).reshape(levels * strip, LANES)
    ones = jnp.ones((levels, 2 * LANES), F32)
    flat = (chunks * levels * strip, LANES)

    def two_rows(ref, c, pair):
        at = c * levels * strip + 2 * pair
        return jnp.concatenate(
            [ref[pl.ds(at + k, levels, stride=strip), :] for k in range(2)], 1
        )

    def slope_rows(at, carry):
        c, pair = lax.div(at, strip // 2), lax.rem(at, strip // 2)
        line = jnp.concatenate([two_rows(path.reshape(flat), c, pair), ones], 0).astype(BF16)
        for m in range(4):
            part = slice(m * hidden // 4, (m + 1) * hidden // 4)
            half_act = dot(w_path[part, :], line)
            bend = jnp.tanh(half_act)
            slopes[at, part, :] = (1.0 + bend) * (1.0 + half_act * (1.0 - bend))
        return carry

    lax.fori_loop(0, chunks * strip // 2, slope_rows, 0)

    def network(source, target, w_first, w_second):
        def visit(at, carry):
            c, pair = lax.div(at, strip // 2), lax.rem(at, strip // 2)
            line = two_rows(source.reshape(flat), c, pair)
            narrow = line.astype(BF16)
            parts = []
            for m in range(4):
                part = slice(m * hidden // 4, (m + 1) * hidden // 4)
                parts.append((slopes[at, part, :] * dot(w_first[part, :], narrow)).astype(BF16))
            line = line + dot(w_second[...], jnp.concatenate(parts, 0))
            for k in range(2):
                row = c * levels * strip + 2 * pair + k
                target.reshape(flat)[pl.ds(row, levels, stride=strip), :] = line[
                    :, k * LANES : (k + 1) * LANES
                ]
            return carry

        return visit

    load_mult.wait()
    exact = lax.Precision.HIGHEST
    left = split_two(dot_nt(row_factor[...], row_factor[...], exact))
    right = split_two(dot_nt(col_factor[...], col_factor[...], exact))

    def correlate(level, carry):
        scale = spread[first + level]
        inner = split_two(dot_three(left, split_two(mult[level])))
        before[level] = (scale * scale) * dot_three(inner, right) + inc[level]
        return carry

    lax.fori_loop(0, depth, correlate, 0)

    for level in range(depth):
        high, low = split_two(inc[level].T)
        part = slice(level * rows, (level + 1) * rows)
        picked[0:cols, part] = high
        picked[cols : 2 * cols, part] = low
    placed[...] = jnp.zeros_like(placed)
    keep_dual.wait()
    for p in PARTNERS:
        dual_copy(p).wait_recv()
    row_ids = lax.broadcasted_iota(jnp.int32, (depth * rows, BLOCK), 0)
    col_ids = lax.broadcasted_iota(jnp.int32, (cols, BLOCK), 0)

    def observe(block, carry):
        here = pl.ds(pl.multiple_of(block * BLOCK, BLOCK), BLOCK)
        local = sites[0:1, here] - first
        inside = (local >= 0) & (local < depth)
        row_at = jnp.where(inside, local * rows + sites[1:2, here], -1)
        hot = jnp.where(row_ids == row_at, 1.0, 0.0).astype(BF16)
        chosen = col_ids == sites[2:3, here]
        value = duals[block]
        high = value.astype(BF16).astype(F32)
        low = value - high
        spots = jnp.concatenate(
            [jnp.where(chosen, high, 0.0).astype(BF16), jnp.where(chosen, low, 0.0).astype(BF16)], 1
        )
        placed[...] += dot_nt(jnp.concatenate([hot, hot], 1), spots)
        found = dot(picked[...], hot)
        found = found[0:cols] + found[cols : 2 * cols]
        seen[block] = jnp.sum(jnp.where(chosen, found, 0.0), axis=0, keepdims=True)
        return carry

    blocks = sites.shape[1] // BLOCK
    cut = blocks // 2

    adjoint = network(strip_m, out_b, w_adjoint, w_in_t)
    tangent = network(strip_i, out_f, w_tangent, w_out)

    @pl.when(has_prior)
    def _():
        for c in range(chunks):
            keep_mult(c).wait()
            for p in PARTNERS:
                mult_copy(p, c).wait_recv()
            lax.fori_loop(c * strip // 2, (c + 1) * strip // 2, adjoint, 0)
            for p in everyone:
                back_copy(p, c).start()

    lax.fori_loop(0, cut, observe, 0)

    @pl.when(has_prior)
    def _():
        for c in range(chunks):
            for p in everyone:
                inc_copy(p, c).wait_recv()
            lax.fori_loop(c * strip // 2, (c + 1) * strip // 2, tangent, 0)
            for p in PARTNERS:
                ahead_copy(p, c).start()
            keep_ahead(c).start()

    lax.fori_loop(cut, blocks, observe, 0)
    for p in PARTNERS:
        seen_copy(p).start()
    keep_seen.start()

    def add_placed(level):
        return mult[level] + placed[pl.ds(pl.multiple_of(level * rows, rows), rows), :]

    @pl.when(has_after)
    def _():
        for c in range(chunks):
            for p in everyone:
                back_copy(p, c).wait_recv()

        def step_back(level, carry):
            at = first + level
            later = stencil(slab_b[level], diffusion[at], drift_rows[at], drift_cols[at], -1.0)
            outm[level] = add_placed(level) - later
            return carry

        lax.fori_loop(0, depth, step_back, 0)

    @pl.when(w == wins - 1)
    def _():
        def plain(level, carry):
            outm[level] = add_placed(level)
            return carry

        lax.fori_loop(0, depth, plain, 0)

    store_mult = pltpu.make_async_copy(outm, mult_out_any, store_sem.at[0])
    store_mult.start()

    keep_seen.wait()
    for p in PARTNERS:
        seen_copy(p).wait_recv()
    obs_out[...] = variance[...] * dual[...] + jnp.sum(seen_in[...], axis=0)

    @pl.when(has_prior)
    def _():
        for c in range(chunks):
            keep_ahead(c).wait()
            for p in PARTNERS:
                ahead_copy(p, c).wait_recv()

        def subtract(level, carry):
            outs[level] = before[level] - slab_f[level]
            return carry

        lax.fori_loop(0, depth, subtract, 0)

    @pl.when(w == 0)
    def _():
        outs[...] = before[...]

    store_state = pltpu.make_async_copy(outs, state_any, store_sem.at[1])
    store_state.start()

    for p in PARTNERS:
        dual_copy(p).wait_send()
        seen_copy(p).wait_send()

    @pl.when(has_prior)
    def _():
        for c in range(chunks):
            for p in everyone:
                back_copy(p, c).wait_send()
            for p in PARTNERS:
                mult_copy(p, c).wait_send()
                ahead_copy(p, c).wait_send()

    @pl.when(has_after)
    def _():
        for c in range(chunks):
            for p in everyone:
                inc_copy(p, c).wait_send()

    store_mult.wait()
    store_state.wait()


def body(
    increment, multiplier, obs_dual, obs_sites, obs_variance, trajectory, diffusion, drift_rows,
    drift_cols, spread, row_factor, col_factor, layer_in, bias_in, layer_out,
):
    _, depth, rows, cols = increment.shape
    _, levels, strip, _ = trajectory.shape
    hidden = layer_in.shape[0]
    own = obs_dual.shape[1]
    spaces = lax.axis_size("space")
    pair = (own // BLOCK, 1, BLOCK)
    slab = pltpu.VMEM((depth, rows, cols), F32)
    chunks = cols // LANES
    row_strip = pltpu.VMEM((chunks, levels, strip, LANES), F32)
    vmem = pl.BlockSpec(memory_space=pltpu.VMEM)
    smem = pl.BlockSpec(memory_space=pltpu.SMEM)
    anywhere = pl.BlockSpec(memory_space=pl.ANY)
    dma = pltpu.SemaphoreType.DMA
    state, seen, mult_out = pl.pallas_call(
        kernel,
        out_shape=(
            jax.ShapeDtypeStruct((depth, rows, cols), F32),
            jax.ShapeDtypeStruct(pair, F32),
            jax.ShapeDtypeStruct((depth, rows, cols), F32),
        ),
        in_specs=[vmem] * 3 + [smem] * 4 + [vmem] * 5 + [anywhere] * 3,
        out_specs=(anywhere, vmem, anywhere),
        scratch_shapes=[
            slab, slab, slab,
            pltpu.VMEM((levels, strip, cols), BF16),
            pltpu.VMEM((chunks, levels * strip, LANES), F32),
            row_strip, row_strip,
            pltpu.VMEM((chunks * strip // 2, hidden, 2 * LANES), F32),
            row_strip, row_strip,
            slab, slab, slab,
            pltpu.VMEM((depth * rows, cols), F32),
            pltpu.VMEM((2 * cols, depth * rows), BF16),
            pltpu.VMEM((hidden, 2 * levels), BF16),
            pltpu.VMEM((hidden, levels), BF16),
            pltpu.VMEM((hidden, levels), BF16),
            pltpu.VMEM((levels, hidden), BF16),
            pltpu.VMEM((spaces * own // BLOCK, 1, BLOCK), F32),
            pltpu.VMEM((spaces * own // BLOCK, 1, BLOCK), F32),
            pltpu.VMEM((spaces,) + pair, F32),
            slab, slab,
            dma((3,)), dma((2,)),
            *[dma((chunks, spaces))] * 8,
            *[dma((spaces,))] * 4,
            dma((2 + 2 * chunks,)),
        ],
        compiler_params=pltpu.CompilerParams(
            collective_id=0, has_side_effects=True, vmem_limit_bytes=60 * 1024 * 1024
        ),
        name="saddle",
    )(
        obs_sites[0], obs_dual.reshape(pair), obs_variance.reshape(pair),
        diffusion, drift_rows, drift_cols, spread, row_factor, col_factor,
        layer_in, bias_in.reshape(1, hidden), layer_out,
        increment[0], multiplier[0], trajectory[0],
    )
    return state[None], seen.reshape(1, own), mult_out[None]


def solution(mesh):
    placed = (
        P("win", "space", None, None), P("win", "space", None, None), P("win", "space"),
        P("win", None, None), P("win", "space"), P("win", None, "space", None),
        P(), P(), P(), P(), P(), P(), P(), P(), P(),
    )
    return jax.shard_map(
        body,
        mesh=mesh,
        in_specs=placed,
        out_specs=(P("win", "space", None, None), P("win", "space"), P("win", "space", None, None)),
        check_vma=False,
    )
```

```python
import jax
import jax.numpy as jnp
from jax import lax
from jax.experimental import pallas as pl
from jax.experimental.pallas import tpu as pltpu
from jax.sharding import PartitionSpec as P

STEPS = 4
MESH = pl.DeviceIdType.MESH
F32, BF16 = jnp.float32, jnp.bfloat16
PARTNERS = (8, 12, 10, 14, 9, 13, 11, 15, 4, 6, 2, 5, 7, 3, 1)
BLOCK = 512
LANES = 128
VMEM_LIMIT = 44 * 1024 * 1024


def flip(value, mask):
    for bit in (1, 2, 4, 8):
        if mask & bit:
            value = value + bit * (1 - 2 * lax.rem(lax.div(value, bit), 2))
    return value


def split_two(value):
    high = value.astype(BF16)
    low = (value - high.astype(F32)).astype(BF16)
    return high, low


def dot(a, b):
    return jnp.dot(a, b, preferred_element_type=F32)


def dot_nt(a, b, precision=None):
    return lax.dot_general(
        a, b, (((1,), (1,)), ((), ())), precision=precision, preferred_element_type=F32
    )


def dot_three(a, b):
    return dot(a[0], b[0]) + (dot(a[0], b[1]) + dot(a[1], b[0]))


def stencil(field, diffusion, drift_rows, drift_cols, direction):
    rows, cols = field.shape
    edge = 8
    row_id = lax.broadcasted_iota(jnp.int32, (edge, cols), 0)
    col_id = lax.broadcasted_iota(jnp.int32, (1, cols), 1)
    centre = 1.0 - 4.0 * diffusion
    row_up, row_dn = diffusion - direction * drift_rows, diffusion + direction * drift_rows
    col_up = jnp.where(col_id == cols - 1, 0.0, diffusion - direction * drift_cols)
    col_dn = jnp.where(col_id == 0, 0.0, diffusion + direction * drift_cols)
    for _ in range(STEPS):
        up1 = pltpu.roll(field, rows - 1, 0)
        last = jnp.where(row_id == edge - 1, 0.0, up1[rows - edge :])
        up1 = jnp.concatenate([up1[: rows - edge], last], 0)
        dn1 = pltpu.roll(field, 1, 0)
        dn1 = jnp.concatenate([jnp.where(row_id == 0, 0.0, dn1[:edge]), dn1[edge:]], 0)
        up2 = pltpu.roll(field, cols - 1, 1)
        dn2 = pltpu.roll(field, 1, 1)
        field = centre * field + (row_up * up1 + row_dn * dn1) + (col_up * up2 + col_dn * dn2)
    return field


def kernel(
    sites_any, dual_any, variance_any, diffusion_any, drift_rows_any, drift_cols_any, spread_any,
    row_any, col_any, w_in_t_any, bias_any, w_out_any, inc_any, mult_any, traj_any,
    before_any, slab_f, obs_any, mult_out_any,
    sites, dual, variance, diffusion, drift_rows, drift_cols, spread, row_factor, col_factor,
    w_in_t, bias, w_out, inc, mult, traj,
    stepped, path, strip_m, strip_i, slopes, out_b, out_f, slab_b,
    before, placed, picked, w_path, w_tangent, w_adjoint, duals, seen, seen_in, outm, obs,
    load_sem, store_sem, m_send, m_recv, i_send, i_recv, b_send, b_recv, f_send, f_recv,
    d_send, d_recv, s_send, s_recv, keep_sem, level_sem,
):
    depth, rows, cols = inc.shape
    chunks, levels, strip, _ = strip_m.shape
    hidden = w_out.shape[1]
    spaces = rows // strip
    w, s = lax.axis_index("win"), lax.axis_index("space")
    wins = lax.axis_size("win")
    after, prior = lax.rem(w + 1, wins), lax.rem(w + wins - 1, wins)
    first = s * depth

    barrier = pltpu.get_barrier_semaphore()
    for p in PARTNERS + (0,):
        d = flip(s, p)
        for win in (w, after, prior):
            if win is w and p == 0:
                continue
            pl.semaphore_signal(
                barrier, inc=1, device_id={"win": win, "space": d}, device_id_type=MESH
            )

    loads = [
        pltpu.make_async_copy(src, dst, load_sem.at[k])
        for k, (src, dst) in enumerate((
            (inc_any, inc), (diffusion_any, diffusion), (drift_rows_any, drift_rows),
            (drift_cols_any, drift_cols), (w_in_t_any, w_in_t), (bias_any, bias),
            (w_out_any, w_out), (traj_any, traj), (mult_any, mult), (spread_any, spread),
            (row_any, row_factor), (col_any, col_factor), (sites_any, sites), (dual_any, dual),
            (variance_any, variance),
        ))
    ]
    for load in loads:
        load.start()
    pl.semaphore_wait(barrier, 3 * spaces - 1)

    def remote(src, dst, send, recv, win, space):
        return pltpu.make_async_remote_copy(
            src_ref=src, dst_ref=dst, send_sem=send, recv_sem=recv,
            device_id={"win": win, "space": space}, device_id_type=MESH,
        )

    def strip_of(d):
        return pl.ds(pl.multiple_of(d * strip, strip), strip)

    def depth_of(d):
        return pl.ds(pl.multiple_of(d * depth, depth), depth)

    def chunk_of(c):
        return pl.ds(c * LANES, LANES)

    def dual_copy(p):
        return remote(dual_any, duals.at[pl.ds(2 * s, 2)], d_send, d_recv, w, flip(s, p))

    def mult_copy(p, c):
        d = flip(s, p)
        return remote(
            mult_any.at[:, strip_of(d), chunk_of(c)], strip_m.at[c, depth_of(s)],
            m_send.at[c], m_recv.at[c], w, d,
        )

    def inc_copy(p, c):
        d = flip(s, p)
        return remote(
            stepped.at[:, strip_of(d), chunk_of(c)], strip_i.at[c, depth_of(s)],
            i_send.at[c], i_recv.at[c], after, d,
        )

    def back_copy(p, c):
        d = flip(s, p)
        return remote(
            out_b.at[c, depth_of(d)], slab_b.at[:, strip_of(s), chunk_of(c)],
            b_send.at[c], b_recv.at[c], prior, d,
        )

    def ahead_copy(p, c):
        d = flip(s, p)
        return remote(
            out_f.at[c, depth_of(d)], slab_f.at[:, strip_of(s), chunk_of(c)],
            f_send.at[c], f_recv.at[c], w, d,
        )

    def seen_copy(p):
        d = flip(s, p)
        return remote(
            seen.at[pl.ds(2 * d, 2)], seen_in.at[s], s_send, s_recv, w, d
        )

    keep_dual = pltpu.make_async_copy(dual_any, duals.at[pl.ds(2 * s, 2)], keep_sem.at[0])
    keep_seen = pltpu.make_async_copy(seen.at[pl.ds(2 * s, 2)], seen_in.at[s], keep_sem.at[1])

    def keep_mult(c):
        return pltpu.make_async_copy(
            mult_any.at[:, strip_of(s), chunk_of(c)], strip_m.at[c, depth_of(s)],
            keep_sem.at[2 + c],
        )

    def keep_ahead(c):
        return pltpu.make_async_copy(
            out_f.at[c, depth_of(s)], slab_f.at[:, strip_of(s), chunk_of(c)],
            keep_sem.at[2 + chunks + c],
        )

    others = spaces - 1

    def all_of(ref, send, recv):
        return remote(ref, ref, send, recv, w, s)

    def all_mult(c):
        return all_of(strip_m.at[c, pl.ds(0, others * depth)], m_send.at[c], m_recv.at[c])

    def all_inc(c):
        return all_of(strip_i.at[c], i_send.at[c], i_recv.at[c])

    def all_back(c):
        return all_of(out_b.at[c], b_send.at[c], b_recv.at[c])

    def all_ahead(c):
        return all_of(out_f.at[c, pl.ds(0, others * depth)], f_send.at[c], f_recv.at[c])

    all_dual = all_of(duals.at[pl.ds(0, others * 2)], d_send, d_recv)
    all_seen = all_of(seen.at[pl.ds(0, others * 2)], s_send, s_recv)
    everyone = PARTNERS + (0,)
    has_prior, has_after = w > 0, w < wins - 1

    keep_dual.start()
    for p in PARTNERS:
        dual_copy(p).start()

    @pl.when(has_prior)
    def _():
        for c in range(chunks):
            for p in PARTNERS:
                mult_copy(p, c).start()
            keep_mult(c).start()

    for load in loads[0:4]:
        load.wait()

    def step_forward(level, carry):
        at = first + level
        stepped[level] = stencil(
            inc[level], diffusion[at], drift_rows[at], drift_cols[at], 1.0
        )
        return carry

    lax.fori_loop(0, depth, step_forward, 0)

    @pl.when(has_after)
    def _():
        for c in range(chunks):
            for p in everyone:
                inc_copy(p, c).start()

    for load in loads[4:8]:
        load.wait()
    lane = lax.broadcasted_iota(jnp.int32, (hidden, 2 * levels), 1)
    bias_all = jnp.broadcast_to(bias[...], (2 * levels, hidden)).T
    bias_hi = bias_all.astype(BF16).astype(F32)
    bias_mid = (bias_all - bias_hi).astype(BF16).astype(F32)
    bias_lo = bias_all - bias_hi - bias_mid
    w_in32 = w_in_t[...].astype(F32).T
    wide = jnp.concatenate([w_in32, jnp.zeros((hidden, levels), F32)], 1)
    wide = jnp.where(lane == levels, bias_hi, wide)
    wide = jnp.where(lane == levels + 1, bias_mid, wide)
    wide = jnp.where(lane == levels + 2, bias_lo, wide)
    w_path[...] = (0.5 * wide).astype(BF16)
    w_tangent[...] = (0.5 * w_in32).astype(BF16)
    w_adjoint[...] = (0.5 * w_out[...].astype(F32).T).astype(BF16)

    for c in range(chunks):
        path[c] = traj[:, :, c * LANES : (c + 1) * LANES].astype(F32).reshape(levels * strip, LANES)
    ones = jnp.ones((levels, 2 * LANES), F32)
    flat = (chunks * levels * strip, LANES)

    def two_rows(ref, c, pair):
        at = c * levels * strip + 2 * pair
        return jnp.concatenate(
            [ref[pl.ds(at + k, levels, stride=strip), :] for k in range(2)], 1
        )

    def slope_rows(at, carry):
        c, pair = lax.div(at, strip // 2), lax.rem(at, strip // 2)
        line = jnp.concatenate([two_rows(path.reshape(flat), c, pair), ones], 0).astype(BF16)
        for m in range(4):
            part = slice(m * hidden // 4, (m + 1) * hidden // 4)
            half_act = dot(w_path[part, :], line)
            bend = jnp.tanh(half_act)
            slopes[at, part, :] = (1.0 + bend) * (1.0 + half_act * (1.0 - bend))
        return carry

    lax.fori_loop(0, chunks * strip // 2, slope_rows, 0)

    def network(source, target, w_first, w_second):
        def visit(at, carry):
            c, pair = lax.div(at, strip // 2), lax.rem(at, strip // 2)
            line = two_rows(source.reshape(flat), c, pair)
            narrow = line.astype(BF16)
            parts = []
            for m in range(4):
                part = slice(m * hidden // 4, (m + 1) * hidden // 4)
                parts.append((slopes[at, part, :] * dot(w_first[part, :], narrow)).astype(BF16))
            line = line + dot(w_second[...], jnp.concatenate(parts, 0))
            for k in range(2):
                row = c * levels * strip + 2 * pair + k
                target.reshape(flat)[pl.ds(row, levels, stride=strip), :] = line[
                    :, k * LANES : (k + 1) * LANES
                ]
            return carry

        return visit

    for load in loads[8:]:
        load.wait()
    exact = lax.Precision.HIGHEST
    left = split_two(dot_nt(row_factor[...], row_factor[...], exact))
    right = split_two(dot_nt(col_factor[...], col_factor[...], exact))

    def correlate(level, carry):
        scale = spread[first + level]
        inner = split_two(dot_three(left, split_two(mult[level])))
        before[level] = (scale * scale) * dot_three(inner, right) + inc[level]
        return carry

    lax.fori_loop(0, depth, correlate, 0)
    store_before = pltpu.make_async_copy(before, before_any, store_sem.at[0])
    store_before.start()

    for level in range(depth):
        high, low = split_two(inc[level].T)
        part = slice(level * rows, (level + 1) * rows)
        picked[0:cols, part] = high
        picked[cols : 2 * cols, part] = low
    placed[...] = jnp.zeros_like(placed)
    keep_dual.wait()
    all_dual.wait_recv()
    row_ids = lax.broadcasted_iota(jnp.int32, (depth * rows, BLOCK), 0)
    col_ids = lax.broadcasted_iota(jnp.int32, (cols, BLOCK), 0)

    def observe(block, carry):
        here = pl.ds(pl.multiple_of(block * BLOCK, BLOCK), BLOCK)
        local = sites[0, :, here] - first
        inside = (local >= 0) & (local < depth)
        row_at = jnp.where(inside, local * rows + sites[1, :, here], -1)
        hot = jnp.where(row_ids == row_at, 1.0, 0.0).astype(BF16)
        chosen = col_ids == sites[2, :, here]
        value = duals[block]
        high = value.astype(BF16).astype(F32)
        low = value - high
        spots = jnp.concatenate(
            [jnp.where(chosen, high, 0.0).astype(BF16), jnp.where(chosen, low, 0.0).astype(BF16)], 1
        )
        placed[...] += dot_nt(jnp.concatenate([hot, hot], 1), spots)
        found = dot(picked[...], hot)
        found = found[0:cols] + found[cols : 2 * cols]
        seen[block] = jnp.sum(jnp.where(chosen, found, 0.0), axis=0, keepdims=True)
        return carry

    blocks = sites.shape[2] // BLOCK
    cuts = [blocks * k // 32 for k in (0, 4, 13, 20, 32)]

    adjoint = network(strip_m, out_b, w_adjoint, w_in_t)
    tangent = network(strip_i, out_f, w_tangent, w_out)

    for c in range(chunks):

        @pl.when(has_prior)
        def _():
            keep_mult(c).wait()
            all_mult(c).wait_recv()
            lax.fori_loop(c * strip // 2, (c + 1) * strip // 2, adjoint, 0)
            for p in everyone:
                back_copy(p, c).start()

        lax.fori_loop(cuts[c], cuts[c + 1], observe, 0)

    for c in range(chunks):

        @pl.when(has_prior)
        def _():
            all_inc(c).wait_recv()
            lax.fori_loop(c * strip // 2, (c + 1) * strip // 2, tangent, 0)
            for p in PARTNERS:
                ahead_copy(p, c).start()
            keep_ahead(c).start()

        lax.fori_loop(cuts[2 + c], cuts[3 + c], observe, 0)

    def store_mult(level):
        return pltpu.make_async_copy(outm.at[level], mult_out_any.at[level], level_sem.at[level])

    for p in PARTNERS:
        seen_copy(p).start()
    keep_seen.start()

    def add_placed(level):
        return mult[level] + placed[pl.ds(pl.multiple_of(level * rows, rows), rows), :]


    @pl.when(has_after)
    def _():
        for c in range(chunks):
            all_back(c).wait_recv()

        def step_back(level, carry):
            at = first + level
            later = stencil(slab_b[level], diffusion[at], drift_rows[at], drift_cols[at], -1.0)
            outm[level] = add_placed(level) - later
            store_mult(level).start()
            return carry

        lax.fori_loop(0, depth, step_back, 0)

    @pl.when(w == wins - 1)
    def _():
        def plain(level, carry):
            outm[level] = add_placed(level)
            store_mult(level).start()
            return carry

        lax.fori_loop(0, depth, plain, 0)

    keep_seen.wait()
    all_seen.wait_recv()
    obs[...] = variance[...] * dual[...] + jnp.sum(seen_in[...], axis=0)
    store_obs = pltpu.make_async_copy(obs, obs_any, store_sem.at[2])
    store_obs.start()

    all_dual.wait_send()
    all_seen.wait_send()
    store_before.wait()

    @pl.when(has_after)
    def _():
        for c in range(chunks):
            all_inc(c).wait_send()

    @pl.when(has_prior)
    def _():
        for c in range(chunks):
            all_back(c).wait_send()
            all_mult(c).wait_send()

    for level in range(depth):
        store_mult(level).wait()
    store_obs.wait()

    @pl.when(has_prior)
    def _():
        for c in range(chunks):
            keep_ahead(c).wait()
            all_ahead(c).wait_recv()
        for c in range(chunks):
            all_ahead(c).wait_send()

    @pl.when(w == 0)
    def _():
        stepped[...] = jnp.zeros_like(stepped)
        blank = pltpu.make_async_copy(stepped, slab_f, store_sem.at[3])
        blank.start()
        blank.wait()


def body(
    increment, multiplier, obs_dual, obs_sites, obs_variance, trajectory, diffusion, drift_rows,
    drift_cols, spread, row_factor, col_factor, layer_in, bias_in, layer_out,
):
    _, depth, rows, cols = increment.shape
    _, levels, strip, _ = trajectory.shape
    hidden = layer_in.shape[0]
    own = obs_dual.shape[1]
    spaces = lax.axis_size("space")
    pair = (own // BLOCK, 1, BLOCK)
    slab = pltpu.VMEM((depth, rows, cols), F32)
    chunks = cols // LANES
    row_strip = pltpu.VMEM((chunks, levels, strip, LANES), F32)
    anywhere = pl.BlockSpec(memory_space=pl.ANY)
    smem = pltpu.SMEM((levels,), F32)
    dma = pltpu.SemaphoreType.DMA
    full = jax.ShapeDtypeStruct((depth, rows, cols), F32)
    before, ahead, seen, mult_out = pl.pallas_call(
        kernel,
        out_shape=(full, full, jax.ShapeDtypeStruct(pair, F32), full),
        in_specs=[anywhere] * 15,
        out_specs=(anywhere,) * 4,
        scratch_shapes=[
            pltpu.VMEM((3, 1, spaces * own), jnp.int32),
            pltpu.VMEM(pair, F32), pltpu.VMEM(pair, F32),
            smem, smem, smem, smem,
            pltpu.VMEM((rows, rows), F32), pltpu.VMEM((cols, cols), F32),
            pltpu.VMEM((levels, hidden), BF16),
            pltpu.VMEM((1, hidden), F32),
            pltpu.VMEM((levels, hidden), BF16),
            slab, slab,
            pltpu.VMEM((levels, strip, cols), BF16),
            slab,
            pltpu.VMEM((chunks, levels * strip, LANES), F32),
            row_strip, row_strip,
            pltpu.VMEM((chunks * strip // 2, hidden, 2 * LANES), F32),
            row_strip, row_strip,
            slab,
            slab,
            pltpu.VMEM((depth * rows, cols), F32),
            pltpu.VMEM((2 * cols, depth * rows), BF16),
            pltpu.VMEM((hidden, 2 * levels), BF16),
            pltpu.VMEM((hidden, levels), BF16),
            pltpu.VMEM((hidden, levels), BF16),
            pltpu.VMEM((spaces * own // BLOCK, 1, BLOCK), F32),
            pltpu.VMEM((spaces * own // BLOCK, 1, BLOCK), F32),
            pltpu.VMEM((spaces,) + pair, F32),
            slab,
            pltpu.VMEM(pair, F32),
            dma((15,)), dma((4,)),
            *[dma((chunks,))] * 8,
            *[dma] * 4,
            dma((2 + 2 * chunks,)), dma((depth,)),
        ],
        compiler_params=pltpu.CompilerParams(
            collective_id=0, has_side_effects=True, vmem_limit_bytes=VMEM_LIMIT
        ),
        name="saddle",
    )(
        *[
            pltpu.with_memory_space_constraint(operand, pltpu.HBM)
            for operand in (
                jnp.swapaxes(obs_sites, 0, 1), obs_dual.reshape(pair), obs_variance.reshape(pair),
                diffusion, drift_rows, drift_cols, spread, row_factor, col_factor,
                layer_in.T, bias_in.reshape(1, hidden), layer_out,
                increment[0], multiplier[0], trajectory[0],
            )
        ]
    )
    return (before - ahead)[None], seen.reshape(1, own), mult_out[None]


def solution(mesh):
    placed = (
        P("win", "space", None, None), P("win", "space", None, None), P("win", "space"),
        P("win", None, None), P("win", "space"), P("win", None, "space", None),
        P(), P(), P(), P(), P(), P(), P(), P(), P(),
    )
    return jax.shard_map(
        body,
        mesh=mesh,
        in_specs=placed,
        out_specs=(P("win", "space", None, None), P("win", "space"), P("win", "space", None, None)),
        check_vma=False,
    )
```

```python
import jax
import jax.numpy as jnp
from jax import lax
from jax.experimental import pallas as pl
from jax.experimental.pallas import tpu as pltpu
from jax.sharding import PartitionSpec as P

STEPS = 4
MESH = pl.DeviceIdType.MESH
F32, BF16 = jnp.float32, jnp.bfloat16
PARTNERS = (8, 12, 10, 14, 9, 13, 11, 15, 4, 6, 2, 5, 7, 3, 1)
BLOCK = 512
LANES = 128
VMEM_LIMIT = 44 * 1024 * 1024


def flip(value, mask):
    for bit in (1, 2, 4, 8):
        if mask & bit:
            value = value + bit * (1 - 2 * lax.rem(lax.div(value, bit), 2))
    return value


def split_two(value):
    high = value.astype(BF16)
    low = (value - high.astype(F32)).astype(BF16)
    return high, low


def dot(a, b):
    return jnp.dot(a, b, preferred_element_type=F32)


def dot_nt(a, b, precision=None):
    return lax.dot_general(
        a, b, (((1,), (1,)), ((), ())), precision=precision, preferred_element_type=F32
    )


def dot_three(a, b):
    return dot(a[0], b[0]) + (dot(a[0], b[1]) + dot(a[1], b[0]))


def stencil(field, pads, diffusion, drift_rows, drift_cols, direction):
    rows = field.shape[0]
    edge = (pads.shape[2] - rows) // 2
    lane = lax.broadcasted_iota(jnp.int32, (1, LANES), 1)
    first, last = lane == 0, lane == LANES - 1
    centre = 1.0 - 4.0 * diffusion
    row_up, row_dn = diffusion - direction * drift_rows, diffusion + direction * drift_rows
    col_up, col_dn = diffusion - direction * drift_cols, diffusion + direction * drift_cols
    up_end, dn_end = jnp.where(last, 0.0, col_up), jnp.where(first, 0.0, col_dn)
    parts = [field[:, :LANES], field[:, LANES:]]
    for step in range(STEPS):
        rows_of = []
        for h in range(2):
            page = pads.at[step % 2, h]
            page[edge : edge + rows, :] = parts[h]
            up1, dn1 = page[edge + 1 : edge + 1 + rows, :], page[edge - 1 : edge - 1 + rows, :]
            rows_of.append(centre * parts[h] + (row_up * up1 + row_dn * dn1))
        ups = [pltpu.roll(part, LANES - 1, 1) for part in parts]
        downs = [pltpu.roll(part, 1, 1) for part in parts]
        parts = [
            rows_of[0] + (col_up * jnp.where(last, ups[1], ups[0]) + dn_end * downs[0]),
            rows_of[1] + (up_end * ups[1] + col_dn * jnp.where(first, downs[0], downs[1])),
        ]
    return jnp.concatenate(parts, 1)


def kernel(
    sites_any, dual_any, variance_any, diffusion_any, drift_rows_any, drift_cols_any, spread_any,
    row_any, col_any, w_in_t_any, bias_any, w_out_any, inc_any, mult_any, traj_any,
    before_any, slab_f, obs_any, mult_out_any,
    sites, dual, variance, diffusion, drift_rows, drift_cols, spread, row_factor, col_factor,
    w_in_t, bias, w_out, inc, mult, traj,
    stepped, path, strip_m, strip_i, slopes, out_b, out_f, slab_b,
    before, placed, picked, w_path, w_tangent, w_adjoint, duals, seen, seen_in, outm, obs, pads,
    load_sem, store_sem, m_send, m_recv, i_send, i_recv, b_send, b_recv, f_send, f_recv,
    d_send, d_recv, s_send, s_recv, keep_sem, level_sem,
):
    depth, rows, cols = inc.shape
    chunks, levels, strip, _ = strip_m.shape
    hidden = w_out.shape[1]
    spaces = rows // strip
    w, s = lax.axis_index("win"), lax.axis_index("space")
    wins = lax.axis_size("win")
    after, prior = lax.rem(w + 1, wins), lax.rem(w + wins - 1, wins)
    first = s * depth

    barrier = pltpu.get_barrier_semaphore()
    for p in PARTNERS + (0,):
        d = flip(s, p)
        for win in (w, after, prior):
            if win is w and p == 0:
                continue
            pl.semaphore_signal(
                barrier, inc=1, device_id={"win": win, "space": d}, device_id_type=MESH
            )

    loads = [
        pltpu.make_async_copy(src, dst, load_sem.at[k])
        for k, (src, dst) in enumerate((
            (inc_any, inc), (diffusion_any, diffusion), (drift_rows_any, drift_rows),
            (drift_cols_any, drift_cols), (w_in_t_any, w_in_t), (bias_any, bias),
            (w_out_any, w_out), (traj_any, traj), (mult_any, mult), (spread_any, spread),
            (row_any, row_factor), (col_any, col_factor), (sites_any, sites), (dual_any, dual),
            (variance_any, variance),
        ))
    ]
    for load in loads:
        load.start()
    pl.semaphore_wait(barrier, 3 * spaces - 1)

    def remote(src, dst, send, recv, win, space):
        return pltpu.make_async_remote_copy(
            src_ref=src, dst_ref=dst, send_sem=send, recv_sem=recv,
            device_id={"win": win, "space": space}, device_id_type=MESH,
        )

    def strip_of(d):
        return pl.ds(pl.multiple_of(d * strip, strip), strip)

    def depth_of(d):
        return pl.ds(pl.multiple_of(d * depth, depth), depth)

    def chunk_of(c):
        return pl.ds(c * LANES, LANES)

    def dual_copy(p):
        return remote(dual_any, duals.at[pl.ds(2 * s, 2)], d_send, d_recv, w, flip(s, p))

    def mult_copy(p, c):
        d = flip(s, p)
        return remote(
            mult_any.at[:, strip_of(d), chunk_of(c)], strip_m.at[c, depth_of(s)],
            m_send.at[c], m_recv.at[c], w, d,
        )

    def inc_copy(p, c):
        d = flip(s, p)
        return remote(
            stepped.at[:, strip_of(d), chunk_of(c)], strip_i.at[c, depth_of(s)],
            i_send.at[c], i_recv.at[c], after, d,
        )

    def back_copy(p, c):
        d = flip(s, p)
        return remote(
            out_b.at[c, depth_of(d)], slab_b.at[:, strip_of(s), chunk_of(c)],
            b_send.at[c], b_recv.at[c], prior, d,
        )

    def ahead_copy(p, c):
        d = flip(s, p)
        return remote(
            out_f.at[c, depth_of(d)], slab_f.at[:, strip_of(s), chunk_of(c)],
            f_send.at[c], f_recv.at[c], w, d,
        )

    def seen_copy(p):
        d = flip(s, p)
        return remote(
            seen.at[pl.ds(2 * d, 2)], seen_in.at[s], s_send, s_recv, w, d
        )

    keep_dual = pltpu.make_async_copy(dual_any, duals.at[pl.ds(2 * s, 2)], keep_sem.at[0])
    keep_seen = pltpu.make_async_copy(seen.at[pl.ds(2 * s, 2)], seen_in.at[s], keep_sem.at[1])

    def keep_mult(c):
        return pltpu.make_async_copy(
            mult_any.at[:, strip_of(s), chunk_of(c)], strip_m.at[c, depth_of(s)],
            keep_sem.at[2 + c],
        )

    def keep_ahead(c):
        return pltpu.make_async_copy(
            out_f.at[c, depth_of(s)], slab_f.at[:, strip_of(s), chunk_of(c)],
            keep_sem.at[2 + chunks + c],
        )

    others = spaces - 1

    def all_of(ref, send, recv):
        return remote(ref, ref, send, recv, w, s)

    def all_mult(c):
        return all_of(strip_m.at[c, pl.ds(0, others * depth)], m_send.at[c], m_recv.at[c])

    def all_inc(c):
        return all_of(strip_i.at[c], i_send.at[c], i_recv.at[c])

    def all_back(c):
        return all_of(out_b.at[c], b_send.at[c], b_recv.at[c])

    def all_ahead(c):
        return all_of(out_f.at[c, pl.ds(0, others * depth)], f_send.at[c], f_recv.at[c])

    all_dual = all_of(duals.at[pl.ds(0, others * 2)], d_send, d_recv)
    all_seen = all_of(seen.at[pl.ds(0, others * 2)], s_send, s_recv)
    everyone = PARTNERS + (0,)
    has_prior, has_after = w > 0, w < wins - 1

    keep_dual.start()
    for p in PARTNERS:
        dual_copy(p).start()

    @pl.when(has_prior)
    def _():
        for c in range(chunks):
            for p in PARTNERS:
                mult_copy(p, c).start()
            keep_mult(c).start()

    pads[...] = jnp.zeros_like(pads)
    for load in loads[0:4]:
        load.wait()

    def step_forward(level, carry):
        at = first + level
        stepped[level] = stencil(
            inc[level], pads, diffusion[at], drift_rows[at], drift_cols[at], 1.0
        )
        return carry

    lax.fori_loop(0, depth, step_forward, 0)

    @pl.when(has_after)
    def _():
        for p in everyone:
            inc_copy(p, 0).start()

    @pl.when(has_after)
    def _():
        for p in everyone:
            inc_copy(p, 1).start()

    for load in loads[4:8]:
        load.wait()
    lane = lax.broadcasted_iota(jnp.int32, (hidden, 2 * levels), 1)
    bias_all = jnp.broadcast_to(bias[...], (2 * levels, hidden)).T
    bias_hi = bias_all.astype(BF16).astype(F32)
    bias_mid = (bias_all - bias_hi).astype(BF16).astype(F32)
    bias_lo = bias_all - bias_hi - bias_mid
    w_in32 = w_in_t[...].astype(F32).T
    wide = jnp.concatenate([w_in32, jnp.zeros((hidden, levels), F32)], 1)
    wide = jnp.where(lane == levels, bias_hi, wide)
    wide = jnp.where(lane == levels + 1, bias_mid, wide)
    wide = jnp.where(lane == levels + 2, bias_lo, wide)
    w_path[...] = (0.5 * wide).astype(BF16)
    w_tangent[...] = (0.5 * w_in32).astype(BF16)
    w_adjoint[...] = (0.5 * w_out[...].astype(F32).T).astype(BF16)

    for c in range(chunks):
        path[c] = traj[:, :, c * LANES : (c + 1) * LANES].astype(F32).reshape(levels * strip, LANES)
    ones = jnp.ones((levels, 2 * LANES), F32)
    flat = (chunks * levels * strip, LANES)

    def two_rows(ref, c, pair):
        at = c * levels * strip + 2 * pair
        return jnp.concatenate(
            [ref[pl.ds(at + k, levels, stride=strip), :] for k in range(2)], 1
        )

    def slope_rows(at, carry):
        c, pair = lax.div(at, strip // 2), lax.rem(at, strip // 2)
        line = jnp.concatenate([two_rows(path.reshape(flat), c, pair), ones], 0).astype(BF16)
        for m in range(4):
            part = slice(m * hidden // 4, (m + 1) * hidden // 4)
            half_act = dot(w_path[part, :], line)
            bend = jnp.tanh(half_act)
            slopes[at, part, :] = (1.0 + bend) * (1.0 + half_act * (1.0 - bend))
        return carry

    lax.fori_loop(0 * strip // 2, (0 + 1) * strip // 2, slope_rows, 0)

    def network(source, target, w_first, w_second):
        def visit(at, carry):
            c, pair = lax.div(at, strip // 2), lax.rem(at, strip // 2)
            line = two_rows(source.reshape(flat), c, pair)
            narrow = line.astype(BF16)
            parts = []
            for m in range(4):
                part = slice(m * hidden // 4, (m + 1) * hidden // 4)
                parts.append((slopes[at, part, :] * dot(w_first[part, :], narrow)).astype(BF16))
            line = line + dot(w_second[...], jnp.concatenate(parts, 0))
            for k in range(2):
                row = c * levels * strip + 2 * pair + k
                target.reshape(flat)[pl.ds(row, levels, stride=strip), :] = line[
                    :, k * LANES : (k + 1) * LANES
                ]
            return carry

        return visit

    row_ids = lax.broadcasted_iota(jnp.int32, (depth * rows, BLOCK), 0)
    col_ids = lax.broadcasted_iota(jnp.int32, (cols, BLOCK), 0)

    def observe(block, carry):
        here = pl.ds(pl.multiple_of(block * BLOCK, BLOCK), BLOCK)
        local = sites[0, :, here] - first
        inside = (local >= 0) & (local < depth)
        row_at = jnp.where(inside, local * rows + sites[1, :, here], -1)
        hot = jnp.where(row_ids == row_at, 1.0, 0.0).astype(BF16)
        chosen = col_ids == sites[2, :, here]
        value = duals[block]
        high = value.astype(BF16).astype(F32)
        low = value - high
        spots = jnp.concatenate(
            [jnp.where(chosen, high, 0.0).astype(BF16), jnp.where(chosen, low, 0.0).astype(BF16)], 1
        )
        placed[...] += dot_nt(jnp.concatenate([hot, hot], 1), spots)
        found = dot(picked[...], hot)
        found = found[0:cols] + found[cols : 2 * cols]
        seen[block] = jnp.sum(jnp.where(chosen, found, 0.0), axis=0, keepdims=True)
        return carry

    blocks = sites.shape[2] // BLOCK
    cuts = [blocks * k // 32 for k in (0, 0, 12, 20, 32)]

    adjoint = network(strip_m, out_b, w_adjoint, w_in_t)
    tangent = network(strip_i, out_f, w_tangent, w_out)

    @pl.when(has_prior)
    def _():
        keep_mult(0).wait()
        all_mult(0).wait_recv()
        lax.fori_loop(0 * strip // 2, (0 + 1) * strip // 2, adjoint, 0)
        for p in everyone:
            back_copy(p, 0).start()

    lax.fori_loop(1 * strip // 2, (1 + 1) * strip // 2, slope_rows, 0)
    for load in loads[8:]:
        load.wait()
    exact = lax.Precision.HIGHEST
    left = split_two(dot_nt(row_factor[...], row_factor[...], exact))
    right = split_two(dot_nt(col_factor[...], col_factor[...], exact))

    def correlate(level, carry):
        scale = spread[first + level]
        inner = split_two(dot_three(left, split_two(mult[level])))
        before[level] = (scale * scale) * dot_three(inner, right) + inc[level]
        return carry

    lax.fori_loop(0, depth, correlate, 0)
    store_before = pltpu.make_async_copy(before, before_any, store_sem.at[0])
    store_before.start()

    for level in range(depth):
        high, low = split_two(inc[level].T)
        part = slice(level * rows, (level + 1) * rows)
        picked[0:cols, part] = high
        picked[cols : 2 * cols, part] = low
    placed[...] = jnp.zeros_like(placed)
    keep_dual.wait()
    all_dual.wait_recv()
    @pl.when(has_prior)
    def _():
        keep_mult(1).wait()
        all_mult(1).wait_recv()
        lax.fori_loop(1 * strip // 2, (1 + 1) * strip // 2, adjoint, 0)
        for p in everyone:
            back_copy(p, 1).start()

    lax.fori_loop(cuts[1], cuts[2], observe, 0)


    @pl.when(has_prior)
    def _():
        all_inc(0).wait_recv()
        lax.fori_loop(0 * strip // 2, (0 + 1) * strip // 2, tangent, 0)

    @pl.when(has_prior)
    def _():
        for p in PARTNERS:
            ahead_copy(p, 0).start()
        keep_ahead(0).start()

    lax.fori_loop(12, 20, observe, 0)

    @pl.when(has_prior)
    def _():
        all_inc(1).wait_recv()
        lax.fori_loop(1 * strip // 2, (1 + 1) * strip // 2, tangent, 0)

    lax.fori_loop(20, 24, observe, 0)

    @pl.when(has_prior)
    def _():
        for p in PARTNERS:
            ahead_copy(p, 1).start()
        keep_ahead(1).start()

    lax.fori_loop(24, 32, observe, 0)

    def store_mult(level):
        return pltpu.make_async_copy(outm.at[level], mult_out_any.at[level], level_sem.at[level])

    for p in PARTNERS:
        seen_copy(p).start()
    keep_seen.start()

    def add_placed(level):
        return mult[level] + placed[pl.ds(pl.multiple_of(level * rows, rows), rows), :]


    @pl.when(has_after)
    def _():
        for c in range(chunks):
            all_back(c).wait_recv()

        def step_back(level, carry):
            at = first + level
            later = stencil(slab_b[level], pads, diffusion[at], drift_rows[at], drift_cols[at], -1.0)
            outm[level] = add_placed(level) - later
            store_mult(level).start()
            return carry

        lax.fori_loop(0, depth, step_back, 0)

    @pl.when(w == wins - 1)
    def _():
        def plain(level, carry):
            outm[level] = add_placed(level)
            store_mult(level).start()
            return carry

        lax.fori_loop(0, depth, plain, 0)

    keep_seen.wait()
    all_seen.wait_recv()
    obs[...] = variance[...] * dual[...] + jnp.sum(seen_in[...], axis=0)
    store_obs = pltpu.make_async_copy(obs, obs_any, store_sem.at[2])
    store_obs.start()

    all_dual.wait_send()
    all_seen.wait_send()
    store_before.wait()

    @pl.when(has_after)
    def _():
        for c in range(chunks):
            all_inc(c).wait_send()

    @pl.when(has_prior)
    def _():
        for c in range(chunks):
            all_back(c).wait_send()
            all_mult(c).wait_send()

    for level in range(depth):
        store_mult(level).wait()
    store_obs.wait()

    @pl.when(has_prior)
    def _():
        for c in range(chunks):
            keep_ahead(c).wait()
            all_ahead(c).wait_recv()
        for c in range(chunks):
            all_ahead(c).wait_send()

    @pl.when(w == 0)
    def _():
        stepped[...] = jnp.zeros_like(stepped)
        blank = pltpu.make_async_copy(stepped, slab_f, store_sem.at[3])
        blank.start()
        blank.wait()


def finish(before, ahead, obs_any, mult_any, state_out, obs_out, mult_out, state, sem):
    depth = state.shape[0]
    copies = [
        pltpu.make_async_copy(mult_any, mult_out.at[0], sem.at[depth]),
        pltpu.make_async_copy(obs_any, obs_out.at[0], sem.at[depth + 1]),
    ]
    for copy in copies:
        copy.start()
    for level in range(depth):
        state[level] = before[level] - ahead[level]
        copies.append(
            pltpu.make_async_copy(state.at[level], state_out.at[0, level], sem.at[level])
        )
        copies[-1].start()
    for copy in copies:
        copy.wait()


def body(
    increment, multiplier, obs_dual, obs_sites, obs_variance, trajectory, diffusion, drift_rows,
    drift_cols, spread, row_factor, col_factor, layer_in, bias_in, layer_out,
):
    _, depth, rows, cols = increment.shape
    _, levels, strip, _ = trajectory.shape
    hidden = layer_in.shape[0]
    own = obs_dual.shape[1]
    spaces = lax.axis_size("space")
    pair = (own // BLOCK, 1, BLOCK)
    slab = pltpu.VMEM((depth, rows, cols), F32)
    chunks = cols // LANES
    row_strip = pltpu.VMEM((chunks, levels, strip, LANES), F32)
    anywhere = pl.BlockSpec(memory_space=pl.ANY)
    smem = pltpu.SMEM((levels,), F32)
    dma = pltpu.SemaphoreType.DMA
    full = jax.ShapeDtypeStruct((depth, rows, cols), F32)
    before, ahead, seen, mult_out = pl.pallas_call(
        kernel,
        out_shape=(full, full, jax.ShapeDtypeStruct(pair, F32), full),
        in_specs=[anywhere] * 15,
        out_specs=(anywhere,) * 4,
        scratch_shapes=[
            pltpu.VMEM((3, 1, spaces * own), jnp.int32),
            pltpu.VMEM(pair, F32), pltpu.VMEM(pair, F32),
            smem, smem, smem, smem,
            pltpu.VMEM((rows, rows), F32), pltpu.VMEM((cols, cols), F32),
            pltpu.VMEM((levels, hidden), BF16),
            pltpu.VMEM((1, hidden), F32),
            pltpu.VMEM((levels, hidden), BF16),
            slab, slab,
            pltpu.VMEM((levels, strip, cols), BF16),
            slab,
            pltpu.VMEM((chunks, levels * strip, LANES), F32),
            row_strip, row_strip,
            pltpu.VMEM((chunks * strip // 2, hidden, 2 * LANES), F32),
            row_strip, row_strip,
            slab,
            slab,
            pltpu.VMEM((depth * rows, cols), F32),
            pltpu.VMEM((2 * cols, depth * rows), BF16),
            pltpu.VMEM((hidden, 2 * levels), BF16),
            pltpu.VMEM((hidden, levels), BF16),
            pltpu.VMEM((hidden, levels), BF16),
            pltpu.VMEM((spaces * own // BLOCK, 1, BLOCK), F32),
            pltpu.VMEM((spaces * own // BLOCK, 1, BLOCK), F32),
            pltpu.VMEM((spaces,) + pair, F32),
            slab,
            pltpu.VMEM(pair, F32),
            pltpu.VMEM((2, 2, rows + 16, LANES), F32),
            dma((15,)), dma((4,)),
            *[dma((chunks,))] * 8,
            *[dma] * 4,
            dma((2 + 2 * chunks,)), dma((depth,)),
        ],
        compiler_params=pltpu.CompilerParams(
            collective_id=0, has_side_effects=True, vmem_limit_bytes=VMEM_LIMIT
        ),
        name="saddle",
    )(
        *[
            pltpu.with_memory_space_constraint(operand, pltpu.HBM)
            for operand in (
                jnp.swapaxes(obs_sites, 0, 1), obs_dual.reshape(pair), obs_variance.reshape(pair),
                diffusion, drift_rows, drift_cols, spread, row_factor, col_factor,
                layer_in.T, bias_in.reshape(1, hidden), layer_out,
                increment[0], multiplier[0], trajectory[0],
            )
        ]
    )
    state_out, obs_out, mult_out = pl.pallas_call(
        finish,
        out_shape=(
            jax.ShapeDtypeStruct(increment.shape, F32),
            jax.ShapeDtypeStruct((1, own // BLOCK, 1, BLOCK), F32),
            jax.ShapeDtypeStruct(increment.shape, F32),
        ),
        in_specs=[pl.BlockSpec(memory_space=pltpu.VMEM)] * 2 + [anywhere] * 2,
        out_specs=(anywhere,) * 3,
        scratch_shapes=[slab, dma((depth + 2,))],
        compiler_params=pltpu.CompilerParams(vmem_limit_bytes=8 * 1024 * 1024),
        name="finish",
    )(before, ahead, seen, mult_out)
    return state_out, obs_out.reshape(1, own), mult_out


def solution(mesh):
    placed = (
        P("win", "space", None, None), P("win", "space", None, None), P("win", "space"),
        P("win", None, None), P("win", "space"), P("win", None, "space", None),
        P(), P(), P(), P(), P(), P(), P(), P(), P(),
    )
    return jax.shard_map(
        body,
        mesh=mesh,
        in_specs=placed,
        out_specs=(P("win", "space", None, None), P("win", "space"), P("win", "space", None, None)),
        check_vma=False,
    )
```

```python
import jax
import jax.numpy as jnp
from jax import lax
from jax.experimental import pallas as pl
from jax.experimental.pallas import tpu as pltpu
from jax.sharding import PartitionSpec as P

STEPS = 4
MESH = pl.DeviceIdType.MESH
F32, BF16 = jnp.float32, jnp.bfloat16
PARTNERS = (8, 12, 10, 14, 9, 13, 11, 15, 4, 6, 2, 5, 7, 3, 1)
BLOCK = 512
GROUPS = 4
LANES = 128
VMEM_LIMIT = 44 * 1024 * 1024


def flip(value, mask):
    for bit in (1, 2, 4, 8):
        if mask & bit:
            value = value + bit * (1 - 2 * lax.rem(lax.div(value, bit), 2))
    return value


def split_two(value):
    high = value.astype(BF16)
    low = (value - high.astype(F32)).astype(BF16)
    return high, low


def dot(a, b):
    return jnp.dot(a, b, preferred_element_type=F32)


def dot_nt(a, b, precision=None):
    return lax.dot_general(
        a, b, (((1,), (1,)), ((), ())), precision=precision, preferred_element_type=F32
    )


def dot_three(a, b):
    return dot(a[0], b[0]) + (dot(a[0], b[1]) + dot(a[1], b[0]))


def stencil(field, pads, diffusion, drift_rows, drift_cols, direction):
    rows = field.shape[0]
    edge = (pads.shape[2] - rows) // 2
    lane = lax.broadcasted_iota(jnp.int32, (1, LANES), 1)
    first, last = lane == 0, lane == LANES - 1
    centre = 1.0 - 4.0 * diffusion
    row_up, row_dn = diffusion - direction * drift_rows, diffusion + direction * drift_rows
    col_up, col_dn = diffusion - direction * drift_cols, diffusion + direction * drift_cols
    up_end, dn_end = jnp.where(last, 0.0, col_up), jnp.where(first, 0.0, col_dn)
    parts = [field[:, :LANES], field[:, LANES:]]
    for step in range(STEPS):
        rows_of = []
        for h in range(2):
            page = pads.at[step % 2, h]
            page[edge : edge + rows, :] = parts[h]
            up1, dn1 = page[edge + 1 : edge + 1 + rows, :], page[edge - 1 : edge - 1 + rows, :]
            rows_of.append(centre * parts[h] + (row_up * up1 + row_dn * dn1))
        ups = [pltpu.roll(part, LANES - 1, 1) for part in parts]
        downs = [pltpu.roll(part, 1, 1) for part in parts]
        parts = [
            rows_of[0] + (col_up * jnp.where(last, ups[1], ups[0]) + dn_end * downs[0]),
            rows_of[1] + (up_end * ups[1] + col_dn * jnp.where(first, downs[0], downs[1])),
        ]
    return jnp.concatenate(parts, 1)


def kernel(
    sites_any, dual_any, variance_any, diffusion_any, drift_rows_any, drift_cols_any, spread_any,
    row_any, col_any, w_in_t_any, bias_any, w_out_any, inc_any, mult_any, traj_any,
    before_any, slab_f, obs_any, mult_out_any,
    sites, dual, variance, diffusion, drift_rows, drift_cols, spread, row_factor, col_factor,
    w_in_t, bias, w_out, inc, mult, traj,
    stepped, path, strip_m, strip_i, slopes, out_b, out_f, slab_b,
    before, placed, picked, w_path, w_tangent, w_adjoint, duals, seen, seen_in, outm, obs, pads,
    load_sem, store_sem, m_send, m_recv, i_send, i_recv, b_send, b_recv, f_send, f_recv,
    d_send, d_recv, s_send, s_recv, keep_sem, level_sem,
):
    depth, rows, cols = inc.shape
    chunks, levels, strip, _ = strip_m.shape
    hidden = w_out.shape[1]
    spaces = rows // strip
    w, s = lax.axis_index("win"), lax.axis_index("space")
    wins = lax.axis_size("win")
    after, prior = lax.rem(w + 1, wins), lax.rem(w + wins - 1, wins)
    first = s * depth
    group = depth // GROUPS

    barrier = pltpu.get_barrier_semaphore()
    for p in PARTNERS + (0,):
        d = flip(s, p)
        for win in (w, after, prior):
            if win is w and p == 0:
                continue
            pl.semaphore_signal(
                barrier, inc=1, device_id={"win": win, "space": d}, device_id_type=MESH
            )

    loads = [
        pltpu.make_async_copy(src, dst, load_sem.at[k])
        for k, (src, dst) in enumerate((
            (inc_any, inc), (diffusion_any, diffusion), (drift_rows_any, drift_rows),
            (drift_cols_any, drift_cols), (w_in_t_any, w_in_t), (bias_any, bias),
            (w_out_any, w_out), (traj_any, traj), (mult_any, mult), (spread_any, spread),
            (row_any, row_factor), (col_any, col_factor), (sites_any, sites), (dual_any, dual),
            (variance_any, variance),
        ))
    ]
    for load in loads:
        load.start()
    pl.semaphore_wait(barrier, 3 * spaces - 1)

    def remote(src, dst, send, recv, win, space):
        return pltpu.make_async_remote_copy(
            src_ref=src, dst_ref=dst, send_sem=send, recv_sem=recv,
            device_id={"win": win, "space": space}, device_id_type=MESH,
        )

    def strip_of(d):
        return pl.ds(pl.multiple_of(d * strip, strip), strip)

    def depth_of(d):
        return pl.ds(pl.multiple_of(d * depth, depth), depth)

    def chunk_of(c):
        return pl.ds(c * LANES, LANES)

    def dual_copy(p):
        return remote(dual_any, duals.at[pl.ds(2 * s, 2)], d_send, d_recv, w, flip(s, p))

    def mult_copy(p, c):
        d = flip(s, p)
        return remote(
            mult_any.at[:, strip_of(d), chunk_of(c)], strip_m.at[c, depth_of(s)],
            m_send.at[c], m_recv.at[c], w, d,
        )

    def inc_copy(p, c):
        d = flip(s, p)
        return remote(
            stepped.at[:, strip_of(d), chunk_of(c)], strip_i.at[c, depth_of(s)],
            i_send.at[c], i_recv.at[c], after, d,
        )

    def back_copy(p, c, g):
        d = flip(s, p)
        return remote(
            out_b.at[c, pl.ds(d * depth + g * group, group)],
            slab_b.at[pl.ds(g * group, group), strip_of(s), chunk_of(c)],
            b_send.at[g, c], b_recv.at[g, c], prior, d,
        )

    def ahead_copy(p, c):
        d = flip(s, p)
        return remote(
            out_f.at[c, depth_of(d)], slab_f.at[:, strip_of(s), chunk_of(c)],
            f_send.at[c], f_recv.at[c], w, d,
        )

    def seen_copy(p):
        d = flip(s, p)
        return remote(
            seen.at[pl.ds(2 * d, 2)], seen_in.at[s], s_send, s_recv, w, d
        )

    keep_dual = pltpu.make_async_copy(dual_any, duals.at[pl.ds(2 * s, 2)], keep_sem.at[0])
    keep_seen = pltpu.make_async_copy(seen.at[pl.ds(2 * s, 2)], seen_in.at[s], keep_sem.at[1])

    def keep_mult(c):
        return pltpu.make_async_copy(
            mult_any.at[:, strip_of(s), chunk_of(c)], strip_m.at[c, depth_of(s)],
            keep_sem.at[2 + c],
        )

    def keep_ahead(c):
        return pltpu.make_async_copy(
            out_f.at[c, depth_of(s)], slab_f.at[:, strip_of(s), chunk_of(c)],
            keep_sem.at[2 + chunks + c],
        )

    others = spaces - 1

    def all_of(ref, send, recv):
        return remote(ref, ref, send, recv, w, s)

    def all_mult(c):
        return all_of(strip_m.at[c, pl.ds(0, others * depth)], m_send.at[c], m_recv.at[c])

    def all_inc(c):
        return all_of(strip_i.at[c], i_send.at[c], i_recv.at[c])

    def all_back(c, g):
        part = out_b.at[c, pl.ds(0, spaces * group)]
        return all_of(part, b_send.at[g, c], b_recv.at[g, c])

    def all_ahead(c):
        return all_of(out_f.at[c, pl.ds(0, others * depth)], f_send.at[c], f_recv.at[c])

    all_dual = all_of(duals.at[pl.ds(0, others * 2)], d_send, d_recv)
    all_seen = all_of(seen.at[pl.ds(0, others * 2)], s_send, s_recv)
    everyone = PARTNERS + (0,)
    has_prior, has_after = w > 0, w < wins - 1

    keep_dual.start()
    for p in PARTNERS:
        dual_copy(p).start()

    @pl.when(has_prior)
    def _():
        for c in range(chunks):
            for p in PARTNERS:
                mult_copy(p, c).start()
            keep_mult(c).start()

    pads[...] = jnp.zeros_like(pads)
    for load in loads[0:4]:
        load.wait()

    def step_forward(level, carry):
        at = first + level
        stepped[level] = stencil(
            inc[level], pads, diffusion[at], drift_rows[at], drift_cols[at], 1.0
        )
        return carry

    lax.fori_loop(0, depth, step_forward, 0)

    @pl.when(has_after)
    def _():
        for p in everyone:
            inc_copy(p, 0).start()

    @pl.when(has_after)
    def _():
        for p in everyone:
            inc_copy(p, 1).start()

    for load in loads[4:8]:
        load.wait()
    lane = lax.broadcasted_iota(jnp.int32, (hidden, 2 * levels), 1)
    bias_all = jnp.broadcast_to(bias[...], (2 * levels, hidden)).T
    bias_hi = bias_all.astype(BF16).astype(F32)
    bias_mid = (bias_all - bias_hi).astype(BF16).astype(F32)
    bias_lo = bias_all - bias_hi - bias_mid
    w_in32 = w_in_t[...].astype(F32).T
    wide = jnp.concatenate([w_in32, jnp.zeros((hidden, levels), F32)], 1)
    wide = jnp.where(lane == levels, bias_hi, wide)
    wide = jnp.where(lane == levels + 1, bias_mid, wide)
    wide = jnp.where(lane == levels + 2, bias_lo, wide)
    w_path[...] = (0.5 * wide).astype(BF16)
    w_tangent[...] = (0.5 * w_in32).astype(BF16)
    w_adjoint[...] = (0.5 * w_out[...].astype(F32).T).astype(BF16)

    for c in range(chunks):
        path[c] = traj[:, :, c * LANES : (c + 1) * LANES].astype(F32).reshape(levels * strip, LANES)
    ones = jnp.ones((levels, 2 * LANES), F32)
    flat = (chunks * levels * strip, LANES)

    def two_rows(ref, c, pair):
        at = c * levels * strip + 2 * pair
        return jnp.concatenate(
            [ref[pl.ds(at + k, levels, stride=strip), :] for k in range(2)], 1
        )

    def slope_rows(at, carry):
        c, pair = lax.div(at, strip // 2), lax.rem(at, strip // 2)
        line = jnp.concatenate([two_rows(path.reshape(flat), c, pair), ones], 0).astype(BF16)
        for m in range(4):
            part = slice(m * hidden // 4, (m + 1) * hidden // 4)
            half_act = dot(w_path[part, :], line)
            bend = jnp.tanh(half_act)
            slopes[at, part, :] = (1.0 + bend) * (1.0 + half_act * (1.0 - bend))
        return carry

    lax.fori_loop(0 * strip // 2, (0 + 1) * strip // 2, slope_rows, 0)

    def network(source, target, w_first, w_second):
        def visit(at, carry):
            c, pair = lax.div(at, strip // 2), lax.rem(at, strip // 2)
            line = two_rows(source.reshape(flat), c, pair)
            narrow = line.astype(BF16)
            parts = []
            for m in range(4):
                part = slice(m * hidden // 4, (m + 1) * hidden // 4)
                parts.append((slopes[at, part, :] * dot(w_first[part, :], narrow)).astype(BF16))
            line = line + dot(w_second[...], jnp.concatenate(parts, 0))
            for k in range(2):
                row = c * levels * strip + 2 * pair + k
                target.reshape(flat)[pl.ds(row, levels, stride=strip), :] = line[
                    :, k * LANES : (k + 1) * LANES
                ]
            return carry

        return visit

    row_ids = lax.broadcasted_iota(jnp.int32, (depth * rows, BLOCK), 0)
    col_ids = lax.broadcasted_iota(jnp.int32, (cols, BLOCK), 0)

    def observe(block, carry):
        here = pl.ds(pl.multiple_of(block * BLOCK, BLOCK), BLOCK)
        local = sites[0, :, here] - first
        inside = (local >= 0) & (local < depth)
        row_at = jnp.where(inside, local * rows + sites[1, :, here], -1)
        hot = jnp.where(row_ids == row_at, 1.0, 0.0).astype(BF16)
        chosen = col_ids == sites[2, :, here]
        value = duals[block]
        high = value.astype(BF16).astype(F32)
        low = value - high
        spots = jnp.concatenate(
            [jnp.where(chosen, high, 0.0).astype(BF16), jnp.where(chosen, low, 0.0).astype(BF16)], 1
        )
        placed[...] += dot_nt(jnp.concatenate([hot, hot], 1), spots)
        found = dot(picked[...], hot)
        found = found[0:cols] + found[cols : 2 * cols]
        seen[block] = jnp.sum(jnp.where(chosen, found, 0.0), axis=0, keepdims=True)
        return carry

    blocks = sites.shape[2] // BLOCK
    cuts = [blocks * k // 32 for k in (0, 0, 12, 20, 32)]

    adjoint = network(strip_m, out_b, w_adjoint, w_in_t)
    tangent = network(strip_i, out_f, w_tangent, w_out)

    @pl.when(has_prior)
    def _():
        keep_mult(0).wait()
        all_mult(0).wait_recv()
        lax.fori_loop(0 * strip // 2, (0 + 1) * strip // 2, adjoint, 0)
        for g in range(GROUPS):
            for p in everyone:
                back_copy(p, 0, g).start()

    lax.fori_loop(1 * strip // 2, (1 + 1) * strip // 2, slope_rows, 0)
    for load in loads[8:]:
        load.wait()
    exact = lax.Precision.HIGHEST
    left = split_two(dot_nt(row_factor[...], row_factor[...], exact))
    right = split_two(dot_nt(col_factor[...], col_factor[...], exact))

    def correlate(level, carry):
        scale = spread[first + level]
        inner = split_two(dot_three(left, split_two(mult[level])))
        before[level] = (scale * scale) * dot_three(inner, right) + inc[level]
        return carry

    lax.fori_loop(0, depth, correlate, 0)
    store_before = pltpu.make_async_copy(before, before_any, store_sem.at[0])
    store_before.start()

    for level in range(depth):
        high, low = split_two(inc[level].T)
        part = slice(level * rows, (level + 1) * rows)
        picked[0:cols, part] = high
        picked[cols : 2 * cols, part] = low
    placed[...] = jnp.zeros_like(placed)
    keep_dual.wait()
    all_dual.wait_recv()
    @pl.when(has_prior)
    def _():
        keep_mult(1).wait()
        all_mult(1).wait_recv()
        lax.fori_loop(1 * strip // 2, (1 + 1) * strip // 2, adjoint, 0)
        for g in range(GROUPS):
            for p in everyone:
                back_copy(p, 1, g).start()

    lax.fori_loop(cuts[1], cuts[2], observe, 0)


    @pl.when(has_prior)
    def _():
        all_inc(0).wait_recv()
        lax.fori_loop(0 * strip // 2, (0 + 1) * strip // 2, tangent, 0)

    @pl.when(has_prior)
    def _():
        for p in PARTNERS:
            ahead_copy(p, 0).start()
        keep_ahead(0).start()

    lax.fori_loop(12, 20, observe, 0)

    @pl.when(has_prior)
    def _():
        all_inc(1).wait_recv()
        lax.fori_loop(1 * strip // 2, (1 + 1) * strip // 2, tangent, 0)

    lax.fori_loop(20, 27, observe, 0)

    @pl.when(has_prior)
    def _():
        for p in PARTNERS:
            ahead_copy(p, 1).start()
        keep_ahead(1).start()

    lax.fori_loop(27, 32, observe, 0)

    def store_mult(level):
        return pltpu.make_async_copy(outm.at[level], mult_out_any.at[level], level_sem.at[level])

    for p in PARTNERS:
        seen_copy(p).start()
    keep_seen.start()

    def add_placed(level):
        return mult[level] + placed[pl.ds(pl.multiple_of(level * rows, rows), rows), :]


    @pl.when(has_after)
    def _():

        def step_back(level, carry):
            at = first + level
            later = stencil(slab_b[level], pads, diffusion[at], drift_rows[at], drift_cols[at], -1.0)
            outm[level] = add_placed(level) - later
            store_mult(level).start()
            return carry

        for g in range(GROUPS):
            for c in range(chunks):
                all_back(c, g).wait_recv()
            lax.fori_loop(g * group, (g + 1) * group, step_back, 0)

    @pl.when(w == wins - 1)
    def _():
        def plain(level, carry):
            outm[level] = add_placed(level)
            store_mult(level).start()
            return carry

        lax.fori_loop(0, depth, plain, 0)

    keep_seen.wait()
    all_seen.wait_recv()
    obs[...] = variance[...] * dual[...] + jnp.sum(seen_in[...], axis=0)
    store_obs = pltpu.make_async_copy(obs, obs_any, store_sem.at[2])
    store_obs.start()

    all_dual.wait_send()
    all_seen.wait_send()
    store_before.wait()

    @pl.when(has_after)
    def _():
        for c in range(chunks):
            all_inc(c).wait_send()

    @pl.when(has_prior)
    def _():
        for c in range(chunks):
            for g in range(GROUPS):
                all_back(c, g).wait_send()
            all_mult(c).wait_send()

    for level in range(depth):
        store_mult(level).wait()
    store_obs.wait()

    @pl.when(has_prior)
    def _():
        for c in range(chunks):
            keep_ahead(c).wait()
            all_ahead(c).wait_recv()
        for c in range(chunks):
            all_ahead(c).wait_send()

    @pl.when(w == 0)
    def _():
        stepped[...] = jnp.zeros_like(stepped)
        blank = pltpu.make_async_copy(stepped, slab_f, store_sem.at[3])
        blank.start()
        blank.wait()


def finish(before, ahead, obs_any, mult_any, state_out, obs_out, mult_out, state, sem):
    depth = state.shape[0]
    copies = [
        pltpu.make_async_copy(mult_any, mult_out.at[0], sem.at[depth]),
        pltpu.make_async_copy(obs_any, obs_out.at[0], sem.at[depth + 1]),
    ]
    for copy in copies:
        copy.start()
    for level in range(depth):
        state[level] = before[level] - ahead[level]
        copies.append(
            pltpu.make_async_copy(state.at[level], state_out.at[0, level], sem.at[level])
        )
        copies[-1].start()
    for copy in copies:
        copy.wait()


def body(
    increment, multiplier, obs_dual, obs_sites, obs_variance, trajectory, diffusion, drift_rows,
    drift_cols, spread, row_factor, col_factor, layer_in, bias_in, layer_out,
):
    _, depth, rows, cols = increment.shape
    _, levels, strip, _ = trajectory.shape
    hidden = layer_in.shape[0]
    own = obs_dual.shape[1]
    spaces = lax.axis_size("space")
    pair = (own // BLOCK, 1, BLOCK)
    slab = pltpu.VMEM((depth, rows, cols), F32)
    chunks = cols // LANES
    row_strip = pltpu.VMEM((chunks, levels, strip, LANES), F32)
    anywhere = pl.BlockSpec(memory_space=pl.ANY)
    smem = pltpu.SMEM((levels,), F32)
    dma = pltpu.SemaphoreType.DMA
    full = jax.ShapeDtypeStruct((depth, rows, cols), F32)
    before, ahead, seen, mult_out = pl.pallas_call(
        kernel,
        out_shape=(full, full, jax.ShapeDtypeStruct(pair, F32), full),
        in_specs=[anywhere] * 15,
        out_specs=(anywhere,) * 4,
        scratch_shapes=[
            pltpu.VMEM((3, 1, spaces * own), jnp.int32),
            pltpu.VMEM(pair, F32), pltpu.VMEM(pair, F32),
            smem, smem, smem, smem,
            pltpu.VMEM((rows, rows), F32), pltpu.VMEM((cols, cols), F32),
            pltpu.VMEM((levels, hidden), BF16),
            pltpu.VMEM((1, hidden), F32),
            pltpu.VMEM((levels, hidden), BF16),
            slab, slab,
            pltpu.VMEM((levels, strip, cols), BF16),
            slab,
            pltpu.VMEM((chunks, levels * strip, LANES), F32),
            row_strip, row_strip,
            pltpu.VMEM((chunks * strip // 2, hidden, 2 * LANES), F32),
            row_strip, row_strip,
            slab,
            slab,
            pltpu.VMEM((depth * rows, cols), F32),
            pltpu.VMEM((2 * cols, depth * rows), BF16),
            pltpu.VMEM((hidden, 2 * levels), BF16),
            pltpu.VMEM((hidden, levels), BF16),
            pltpu.VMEM((hidden, levels), BF16),
            pltpu.VMEM((spaces * own // BLOCK, 1, BLOCK), F32),
            pltpu.VMEM((spaces * own // BLOCK, 1, BLOCK), F32),
            pltpu.VMEM((spaces,) + pair, F32),
            slab,
            pltpu.VMEM(pair, F32),
            pltpu.VMEM((2, 2, rows + 16, LANES), F32),
            dma((15,)), dma((4,)),
            *[dma((chunks,))] * 4,
            *[dma((GROUPS, chunks))] * 2,
            *[dma((chunks,))] * 2,
            *[dma] * 4,
            dma((2 + 2 * chunks,)), dma((depth,)),
        ],
        compiler_params=pltpu.CompilerParams(
            collective_id=0, has_side_effects=True, vmem_limit_bytes=VMEM_LIMIT
        ),
        name="saddle",
    )(
        *[
            pltpu.with_memory_space_constraint(operand, pltpu.HBM)
            for operand in (
                jnp.swapaxes(obs_sites, 0, 1), obs_dual.reshape(pair), obs_variance.reshape(pair),
                diffusion, drift_rows, drift_cols, spread, row_factor, col_factor,
                layer_in.T, bias_in.reshape(1, hidden), layer_out,
                increment[0], multiplier[0], trajectory[0],
            )
        ]
    )
    state_out, obs_out, mult_out = pl.pallas_call(
        finish,
        out_shape=(
            jax.ShapeDtypeStruct(increment.shape, F32),
            jax.ShapeDtypeStruct((1, own // BLOCK, 1, BLOCK), F32),
            jax.ShapeDtypeStruct(increment.shape, F32),
        ),
        in_specs=[pl.BlockSpec(memory_space=pltpu.VMEM)] * 2 + [anywhere] * 2,
        out_specs=(anywhere,) * 3,
        scratch_shapes=[slab, dma((depth + 2,))],
        compiler_params=pltpu.CompilerParams(vmem_limit_bytes=8 * 1024 * 1024),
        name="finish",
    )(before, ahead, seen, mult_out)
    return state_out, obs_out.reshape(1, own), mult_out


def solution(mesh):
    placed = (
        P("win", "space", None, None), P("win", "space", None, None), P("win", "space"),
        P("win", None, None), P("win", "space"), P("win", None, "space", None),
        P(), P(), P(), P(), P(), P(), P(), P(), P(),
    )
    return jax.shard_map(
        body,
        mesh=mesh,
        in_specs=placed,
        out_specs=(P("win", "space", None, None), P("win", "space"), P("win", "space", None, None)),
        check_vma=False,
    )
```

```python
import jax
import jax.numpy as jnp
from jax import lax
from jax.experimental import pallas as pl
from jax.experimental.pallas import tpu as pltpu
from jax.sharding import PartitionSpec as P

STEPS = 4
MESH = pl.DeviceIdType.MESH
F32, BF16 = jnp.float32, jnp.bfloat16
PARTNERS = (8, 12, 10, 14, 9, 13, 11, 15, 4, 6, 2, 5, 7, 3, 1)
BLOCK = 512
GROUPS = 4
LANES = 128
VMEM_LIMIT = 44 * 1024 * 1024


def flip(value, mask):
    for bit in (1, 2, 4, 8):
        if mask & bit:
            value = value + bit * (1 - 2 * lax.rem(lax.div(value, bit), 2))
    return value


def split_two(value):
    high = value.astype(BF16)
    low = (value - high.astype(F32)).astype(BF16)
    return high, low


def dot(a, b):
    return jnp.dot(a, b, preferred_element_type=F32)


def dot_nt(a, b, precision=None):
    return lax.dot_general(
        a, b, (((1,), (1,)), ((), ())), precision=precision, preferred_element_type=F32
    )


def dot_three(a, b):
    return dot(a[0], b[0]) + (dot(a[0], b[1]) + dot(a[1], b[0]))


def stencil(field, pads, diffusion, drift_rows, drift_cols, direction):
    rows = field.shape[0]
    edge = (pads.shape[2] - rows) // 2
    lane = lax.broadcasted_iota(jnp.int32, (1, LANES), 1)
    first, last = lane == 0, lane == LANES - 1
    centre = 1.0 - 4.0 * diffusion
    row_up, row_dn = diffusion - direction * drift_rows, diffusion + direction * drift_rows
    col_up, col_dn = diffusion - direction * drift_cols, diffusion + direction * drift_cols
    up_end, dn_end = jnp.where(last, 0.0, col_up), jnp.where(first, 0.0, col_dn)
    parts = [field[:, :LANES], field[:, LANES:]]
    for step in range(STEPS):
        rows_of = []
        for h in range(2):
            page = pads.at[step % 2, h]
            page[edge : edge + rows, :] = parts[h]
            up1, dn1 = page[edge + 1 : edge + 1 + rows, :], page[edge - 1 : edge - 1 + rows, :]
            rows_of.append(centre * parts[h] + (row_up * up1 + row_dn * dn1))
        ups = [pltpu.roll(part, LANES - 1, 1) for part in parts]
        downs = [pltpu.roll(part, 1, 1) for part in parts]
        parts = [
            rows_of[0] + (col_up * jnp.where(last, ups[1], ups[0]) + dn_end * downs[0]),
            rows_of[1] + (up_end * ups[1] + col_dn * jnp.where(first, downs[0], downs[1])),
        ]
    return jnp.concatenate(parts, 1)


def kernel(
    sites_any, dual_any, variance_any, diffusion_any, drift_rows_any, drift_cols_any, spread_any,
    row_any, col_any, w_in_t_any, bias_any, w_out_any, inc_any, mult_any, traj_any,
    before_any, slab_f, obs_any, mult_out_any,
    sites, dual, variance, diffusion, drift_rows, drift_cols, spread, row_factor, col_factor,
    w_in_t, bias, w_out, inc, mult, traj,
    stepped, path, strip_m, strip_i, slopes, out_b, out_f, slab_b,
    before, placed, picked, w_path, w_tangent, w_adjoint, duals, seen, seen_in, outm, obs, pads,
    load_sem, store_sem, m_send, m_recv, i_send, i_recv, b_send, b_recv, f_send, f_recv,
    d_send, d_recv, s_send, s_recv, keep_sem, level_sem,
):
    depth, rows, cols = inc.shape
    chunks, levels, strip, _ = strip_m.shape
    hidden = w_out.shape[1]
    spaces = rows // strip
    w, s = lax.axis_index("win"), lax.axis_index("space")
    wins = lax.axis_size("win")
    after, prior = lax.rem(w + 1, wins), lax.rem(w + wins - 1, wins)
    first = s * depth
    group = depth // GROUPS

    barrier = pltpu.get_barrier_semaphore()
    for p in PARTNERS + (0,):
        d = flip(s, p)
        for win in (w, after, prior):
            if win is w and p == 0:
                continue
            pl.semaphore_signal(
                barrier, inc=1, device_id={"win": win, "space": d}, device_id_type=MESH
            )

    loads = [
        pltpu.make_async_copy(src, dst, load_sem.at[k])
        for k, (src, dst) in enumerate((
            (inc_any, inc), (diffusion_any, diffusion), (drift_rows_any, drift_rows),
            (drift_cols_any, drift_cols), (w_in_t_any, w_in_t), (bias_any, bias),
            (w_out_any, w_out), (traj_any, traj), (mult_any, mult), (spread_any, spread),
            (row_any, row_factor), (col_any, col_factor), (sites_any, sites), (dual_any, dual),
            (variance_any, variance),
        ))
    ]
    for load in loads:
        load.start()
    pl.semaphore_wait(barrier, 3 * spaces - 1)

    def remote(src, dst, send, recv, win, space):
        return pltpu.make_async_remote_copy(
            src_ref=src, dst_ref=dst, send_sem=send, recv_sem=recv,
            device_id={"win": win, "space": space}, device_id_type=MESH,
        )

    def strip_of(d):
        return pl.ds(pl.multiple_of(d * strip, strip), strip)

    def depth_of(d):
        return pl.ds(pl.multiple_of(d * depth, depth), depth)

    def chunk_of(c):
        return pl.ds(c * LANES, LANES)

    def dual_copy(p):
        return remote(dual_any, duals.at[pl.ds(2 * s, 2)], d_send, d_recv, w, flip(s, p))

    def mult_copy(p, c):
        d = flip(s, p)
        return remote(
            mult_any.at[:, strip_of(d), chunk_of(c)], strip_m.at[c, depth_of(s)],
            m_send.at[c], m_recv.at[c], w, d,
        )

    def inc_copy(p, c):
        d = flip(s, p)
        return remote(
            stepped.at[:, strip_of(d), chunk_of(c)], strip_i.at[c, depth_of(s)],
            i_send.at[c], i_recv.at[c], after, d,
        )

    def back_copy(p, c, g):
        d = flip(s, p)
        return remote(
            out_b.at[c, pl.ds(d * depth + g * group, group)],
            slab_b.at[pl.ds(g * group, group), strip_of(s), chunk_of(c)],
            b_send.at[g, c], b_recv.at[g, c], prior, d,
        )

    def ahead_copy(p, c):
        d = flip(s, p)
        return remote(
            out_f.at[c, depth_of(d)], slab_f.at[:, strip_of(s), chunk_of(c)],
            f_send.at[c], f_recv.at[c], w, d,
        )

    def seen_copy(p):
        d = flip(s, p)
        return remote(
            seen.at[pl.ds(2 * d, 2)], seen_in.at[s], s_send, s_recv, w, d
        )

    keep_dual = pltpu.make_async_copy(dual_any, duals.at[pl.ds(2 * s, 2)], keep_sem.at[0])
    keep_seen = pltpu.make_async_copy(seen.at[pl.ds(2 * s, 2)], seen_in.at[s], keep_sem.at[1])

    def keep_mult(c):
        return pltpu.make_async_copy(
            mult_any.at[:, strip_of(s), chunk_of(c)], strip_m.at[c, depth_of(s)],
            keep_sem.at[2 + c],
        )

    def keep_ahead(c):
        return pltpu.make_async_copy(
            out_f.at[c, depth_of(s)], slab_f.at[:, strip_of(s), chunk_of(c)],
            keep_sem.at[2 + chunks + c],
        )

    others = spaces - 1

    def all_of(ref, send, recv):
        return remote(ref, ref, send, recv, w, s)

    def all_mult(c):
        return all_of(strip_m.at[c, pl.ds(0, others * depth)], m_send.at[c], m_recv.at[c])

    def all_inc(c):
        return all_of(strip_i.at[c], i_send.at[c], i_recv.at[c])

    def all_back(c, g):
        part = out_b.at[c, pl.ds(0, spaces * group)]
        return all_of(part, b_send.at[g, c], b_recv.at[g, c])

    def all_ahead(c):
        return all_of(out_f.at[c, pl.ds(0, others * depth)], f_send.at[c], f_recv.at[c])

    all_dual = all_of(duals.at[pl.ds(0, others * 2)], d_send, d_recv)
    all_seen = all_of(seen.at[pl.ds(0, others * 2)], s_send, s_recv)
    everyone = PARTNERS + (0,)
    has_prior, has_after = w > 0, w < wins - 1

    keep_dual.start()

    @pl.when(has_prior)
    def _():
        for c in range(chunks):
            for p in PARTNERS:
                mult_copy(p, c).start()
            keep_mult(c).start()

    for p in PARTNERS:
        dual_copy(p).start()

    pads[...] = jnp.zeros_like(pads)
    for load in loads[0:4]:
        load.wait()

    def step_forward(level, carry):
        at = first + level
        stepped[level] = stencil(
            inc[level], pads, diffusion[at], drift_rows[at], drift_cols[at], 1.0
        )
        return carry

    lax.fori_loop(0, depth, step_forward, 0)

    @pl.when(has_after)
    def _():
        for p in everyone:
            inc_copy(p, 0).start()

    @pl.when(has_after)
    def _():
        for p in everyone:
            inc_copy(p, 1).start()

    for load in loads[4:8]:
        load.wait()
    lane = lax.broadcasted_iota(jnp.int32, (hidden, 2 * levels), 1)
    bias_all = jnp.broadcast_to(bias[...], (2 * levels, hidden)).T
    bias_hi = bias_all.astype(BF16).astype(F32)
    bias_mid = (bias_all - bias_hi).astype(BF16).astype(F32)
    bias_lo = bias_all - bias_hi - bias_mid
    w_in32 = w_in_t[...].astype(F32).T
    wide = jnp.concatenate([w_in32, jnp.zeros((hidden, levels), F32)], 1)
    wide = jnp.where(lane == levels, bias_hi, wide)
    wide = jnp.where(lane == levels + 1, bias_mid, wide)
    wide = jnp.where(lane == levels + 2, bias_lo, wide)
    w_path[...] = (0.5 * wide).astype(BF16)
    w_tangent[...] = (0.5 * w_in32).astype(BF16)
    w_adjoint[...] = (0.5 * w_out[...].astype(F32).T).astype(BF16)

    for c in range(chunks):
        path[c] = traj[:, :, c * LANES : (c + 1) * LANES].astype(F32).reshape(levels * strip, LANES)
    ones = jnp.ones((levels, 2 * LANES), F32)
    flat = (chunks * levels * strip, LANES)

    def two_rows(ref, c, pair):
        at = c * levels * strip + 2 * pair
        return jnp.concatenate(
            [ref[pl.ds(at + k, levels, stride=strip), :] for k in range(2)], 1
        )

    def slope_rows(at, carry):
        c, pair = lax.div(at, strip // 2), lax.rem(at, strip // 2)
        line = jnp.concatenate([two_rows(path.reshape(flat), c, pair), ones], 0).astype(BF16)
        for m in range(4):
            part = slice(m * hidden // 4, (m + 1) * hidden // 4)
            half_act = dot(w_path[part, :], line)
            bend = jnp.tanh(half_act)
            slopes[at, part, :] = (1.0 + bend) * (1.0 + half_act * (1.0 - bend))
        return carry

    lax.fori_loop(0 * strip // 2, (0 + 1) * strip // 2, slope_rows, 0)

    def network(source, target, w_first, w_second):
        def visit(at, carry):
            c, pair = lax.div(at, strip // 2), lax.rem(at, strip // 2)
            line = two_rows(source.reshape(flat), c, pair)
            narrow = line.astype(BF16)
            parts = []
            for m in range(4):
                part = slice(m * hidden // 4, (m + 1) * hidden // 4)
                parts.append((slopes[at, part, :] * dot(w_first[part, :], narrow)).astype(BF16))
            line = line + dot(w_second[...], jnp.concatenate(parts, 0))
            for k in range(2):
                row = c * levels * strip + 2 * pair + k
                target.reshape(flat)[pl.ds(row, levels, stride=strip), :] = line[
                    :, k * LANES : (k + 1) * LANES
                ]
            return carry

        return visit

    row_ids = lax.broadcasted_iota(jnp.int32, (depth * rows, BLOCK), 0)
    col_ids = lax.broadcasted_iota(jnp.int32, (cols, BLOCK), 0)

    def observe(block, carry):
        here = pl.ds(pl.multiple_of(block * BLOCK, BLOCK), BLOCK)
        local = sites[0, :, here] - first
        inside = (local >= 0) & (local < depth)
        row_at = jnp.where(inside, local * rows + sites[1, :, here], -1)
        hot = jnp.where(row_ids == row_at, 1.0, 0.0).astype(BF16)
        chosen = col_ids == sites[2, :, here]
        value = duals[block]
        high = value.astype(BF16).astype(F32)
        low = value - high
        spots = jnp.concatenate(
            [jnp.where(chosen, high, 0.0).astype(BF16), jnp.where(chosen, low, 0.0).astype(BF16)], 1
        )
        placed[...] += dot_nt(jnp.concatenate([hot, hot], 1), spots)
        found = dot(picked[...], hot)
        found = found[0:cols] + found[cols : 2 * cols]
        seen[block] = jnp.sum(jnp.where(chosen, found, 0.0), axis=0, keepdims=True)
        return carry

    blocks = sites.shape[2] // BLOCK
    cuts = [blocks * k // 32 for k in (0, 0, 12, 20, 32)]

    adjoint = network(strip_m, out_b, w_adjoint, w_in_t)
    tangent = network(strip_i, out_f, w_tangent, w_out)

    @pl.when(has_prior)
    def _():
        keep_mult(0).wait()
        all_mult(0).wait_recv()
        lax.fori_loop(0 * strip // 2, (0 + 1) * strip // 2, adjoint, 0)
        for g in range(GROUPS):
            for p in everyone:
                back_copy(p, 0, g).start()

    lax.fori_loop(1 * strip // 2, (1 + 1) * strip // 2, slope_rows, 0)
    for load in loads[8:]:
        load.wait()
    exact = lax.Precision.HIGHEST
    left = split_two(dot_nt(row_factor[...], row_factor[...], exact))
    right = split_two(dot_nt(col_factor[...], col_factor[...], exact))

    def correlate(level, carry):
        scale = spread[first + level]
        inner = split_two(dot_three(left, split_two(mult[level])))
        before[level] = (scale * scale) * dot_three(inner, right) + inc[level]
        return carry

    lax.fori_loop(0, depth, correlate, 0)
    store_before = pltpu.make_async_copy(before, before_any, store_sem.at[0])
    store_before.start()

    for level in range(depth):
        high, low = split_two(inc[level].T)
        part = slice(level * rows, (level + 1) * rows)
        picked[0:cols, part] = high
        picked[cols : 2 * cols, part] = low
    placed[...] = jnp.zeros_like(placed)
    keep_dual.wait()
    all_dual.wait_recv()
    @pl.when(has_prior)
    def _():
        keep_mult(1).wait()
        all_mult(1).wait_recv()
        lax.fori_loop(1 * strip // 2, (1 + 1) * strip // 2, adjoint, 0)
        for g in range(GROUPS):
            for p in everyone:
                back_copy(p, 1, g).start()

    lax.fori_loop(cuts[1], cuts[2], observe, 0)


    @pl.when(has_prior)
    def _():
        all_inc(0).wait_recv()
        lax.fori_loop(0 * strip // 2, (0 + 1) * strip // 2, tangent, 0)

    @pl.when(has_prior)
    def _():
        for p in PARTNERS:
            ahead_copy(p, 0).start()
        keep_ahead(0).start()

    lax.fori_loop(12, 20, observe, 0)

    @pl.when(has_prior)
    def _():
        all_inc(1).wait_recv()
        lax.fori_loop(1 * strip // 2, (1 + 1) * strip // 2, tangent, 0)

    lax.fori_loop(20, 27, observe, 0)

    @pl.when(has_prior)
    def _():
        for p in PARTNERS:
            ahead_copy(p, 1).start()
        keep_ahead(1).start()

    lax.fori_loop(27, 32, observe, 0)

    def store_mult(level):
        return pltpu.make_async_copy(outm.at[level], mult_out_any.at[level], level_sem.at[level])

    for p in PARTNERS:
        seen_copy(p).start()
    keep_seen.start()

    def add_placed(level):
        return mult[level] + placed[pl.ds(pl.multiple_of(level * rows, rows), rows), :]


    @pl.when(has_after)
    def _():

        def step_back(level, carry):
            at = first + level
            later = stencil(slab_b[level], pads, diffusion[at], drift_rows[at], drift_cols[at], -1.0)
            outm[level] = add_placed(level) - later
            store_mult(level).start()
            return carry

        for g in range(GROUPS):
            for c in range(chunks):
                all_back(c, g).wait_recv()
            lax.fori_loop(g * group, (g + 1) * group, step_back, 0)

    @pl.when(w == wins - 1)
    def _():
        def plain(level, carry):
            outm[level] = add_placed(level)
            store_mult(level).start()
            return carry

        lax.fori_loop(0, depth, plain, 0)

    keep_seen.wait()
    all_seen.wait_recv()
    obs[...] = variance[...] * dual[...] + jnp.sum(seen_in[...], axis=0)
    store_obs = pltpu.make_async_copy(obs, obs_any, store_sem.at[2])
    store_obs.start()

    all_dual.wait_send()
    all_seen.wait_send()
    store_before.wait()

    @pl.when(has_after)
    def _():
        for c in range(chunks):
            all_inc(c).wait_send()

    @pl.when(has_prior)
    def _():
        for c in range(chunks):
            for g in range(GROUPS):
                all_back(c, g).wait_send()
            all_mult(c).wait_send()

    for level in range(depth):
        store_mult(level).wait()
    store_obs.wait()

    @pl.when(has_prior)
    def _():
        for c in range(chunks):
            keep_ahead(c).wait()
            all_ahead(c).wait_recv()
        for c in range(chunks):
            all_ahead(c).wait_send()

    @pl.when(w == 0)
    def _():
        stepped[...] = jnp.zeros_like(stepped)
        blank = pltpu.make_async_copy(stepped, slab_f, store_sem.at[3])
        blank.start()
        blank.wait()


def finish(before, ahead, obs_any, mult_any, state_out, obs_out, mult_out, state, sem):
    depth = state.shape[0]
    copies = [
        pltpu.make_async_copy(mult_any, mult_out.at[0], sem.at[depth]),
        pltpu.make_async_copy(obs_any, obs_out.at[0], sem.at[depth + 1]),
    ]
    for copy in copies:
        copy.start()
    for level in range(depth):
        state[level] = before[level] - ahead[level]
        copies.append(
            pltpu.make_async_copy(state.at[level], state_out.at[0, level], sem.at[level])
        )
        copies[-1].start()
    for copy in copies:
        copy.wait()


def body(
    increment, multiplier, obs_dual, obs_sites, obs_variance, trajectory, diffusion, drift_rows,
    drift_cols, spread, row_factor, col_factor, layer_in, bias_in, layer_out,
):
    _, depth, rows, cols = increment.shape
    _, levels, strip, _ = trajectory.shape
    hidden = layer_in.shape[0]
    own = obs_dual.shape[1]
    spaces = lax.axis_size("space")
    pair = (own // BLOCK, 1, BLOCK)
    slab = pltpu.VMEM((depth, rows, cols), F32)
    chunks = cols // LANES
    row_strip = pltpu.VMEM((chunks, levels, strip, LANES), F32)
    anywhere = pl.BlockSpec(memory_space=pl.ANY)
    smem = pltpu.SMEM((levels,), F32)
    dma = pltpu.SemaphoreType.DMA
    full = jax.ShapeDtypeStruct((depth, rows, cols), F32)
    before, ahead, seen, mult_out = pl.pallas_call(
        kernel,
        out_shape=(full, full, jax.ShapeDtypeStruct(pair, F32), full),
        in_specs=[anywhere] * 15,
        out_specs=(anywhere,) * 4,
        scratch_shapes=[
            pltpu.VMEM((3, 1, spaces * own), jnp.int32),
            pltpu.VMEM(pair, F32), pltpu.VMEM(pair, F32),
            smem, smem, smem, smem,
            pltpu.VMEM((rows, rows), F32), pltpu.VMEM((cols, cols), F32),
            pltpu.VMEM((levels, hidden), BF16),
            pltpu.VMEM((1, hidden), F32),
            pltpu.VMEM((levels, hidden), BF16),
            slab, slab,
            pltpu.VMEM((levels, strip, cols), BF16),
            slab,
            pltpu.VMEM((chunks, levels * strip, LANES), F32),
            row_strip, row_strip,
            pltpu.VMEM((chunks * strip // 2, hidden, 2 * LANES), F32),
            row_strip, row_strip,
            slab,
            slab,
            pltpu.VMEM((depth * rows, cols), F32),
            pltpu.VMEM((2 * cols, depth * rows), BF16),
            pltpu.VMEM((hidden, 2 * levels), BF16),
            pltpu.VMEM((hidden, levels), BF16),
            pltpu.VMEM((hidden, levels), BF16),
            pltpu.VMEM((spaces * own // BLOCK, 1, BLOCK), F32),
            pltpu.VMEM((spaces * own // BLOCK, 1, BLOCK), F32),
            pltpu.VMEM((spaces,) + pair, F32),
            slab,
            pltpu.VMEM(pair, F32),
            pltpu.VMEM((2, 2, rows + 16, LANES), F32),
            dma((15,)), dma((4,)),
            *[dma((chunks,))] * 4,
            *[dma((GROUPS, chunks))] * 2,
            *[dma((chunks,))] * 2,
            *[dma] * 4,
            dma((2 + 2 * chunks,)), dma((depth,)),
        ],
        compiler_params=pltpu.CompilerParams(
            collective_id=0, has_side_effects=True, vmem_limit_bytes=VMEM_LIMIT
        ),
        name="saddle",
    )(
        *[
            pltpu.with_memory_space_constraint(operand, pltpu.HBM)
            for operand in (
                jnp.swapaxes(obs_sites, 0, 1), obs_dual.reshape(pair), obs_variance.reshape(pair),
                diffusion, drift_rows, drift_cols, spread, row_factor, col_factor,
                layer_in.T, bias_in.reshape(1, hidden), layer_out,
                increment[0], multiplier[0], trajectory[0],
            )
        ]
    )
    state_out, obs_out, mult_out = pl.pallas_call(
        finish,
        out_shape=(
            jax.ShapeDtypeStruct(increment.shape, F32),
            jax.ShapeDtypeStruct((1, own // BLOCK, 1, BLOCK), F32),
            jax.ShapeDtypeStruct(increment.shape, F32),
        ),
        in_specs=[pl.BlockSpec(memory_space=pltpu.VMEM)] * 2 + [anywhere] * 2,
        out_specs=(anywhere,) * 3,
        scratch_shapes=[slab, dma((depth + 2,))],
        compiler_params=pltpu.CompilerParams(vmem_limit_bytes=8 * 1024 * 1024),
        name="finish",
    )(before, ahead, seen, mult_out)
    return state_out, obs_out.reshape(1, own), mult_out


def solution(mesh):
    placed = (
        P("win", "space", None, None), P("win", "space", None, None), P("win", "space"),
        P("win", None, None), P("win", "space"), P("win", None, "space", None),
        P(), P(), P(), P(), P(), P(), P(), P(), P(),
    )
    return jax.shard_map(
        body,
        mesh=mesh,
        in_specs=placed,
        out_specs=(P("win", "space", None, None), P("win", "space"), P("win", "space", None, None)),
        check_vma=False,
    )
```
